512 devices in a mesh: dp: 8 (over x, core), context: 64 (over y, z).
Axes of the slice: x: 4, y: 8, z: 8, core: 2. Of those that a mesh axis runs over, the one named last changes fastest.
Arguments:
- queries: bfloat16 [8, 8192, 2048], P('dp', 'context'), may hold values from -6 to 6
- key_rows: bfloat16 [8, 8192, 2048], P('dp', 'context'), may hold values from -6 to 6
- value_rows: bfloat16 [8, 8192, 2048], P('dp', 'context'), may hold values from -6 to 6
- out_grad: bfloat16 [8, 8192, 2048], P('dp', 'context'), may hold values from -6 to 6
- feature_maps: bfloat16 [16, 128, 128], replicated, may hold values from -0.5 to 0.5
Outputs:
- query_grad: bfloat16 [8, 8192, 2048], P('dp', 'context')
- key_grad: bfloat16 [8, 8192, 2048], P('dp', 'context')
- value_grad: bfloat16 [8, 8192, 2048], P('dp', 'context')
- maps_grad: float32 [2048, 128], P(('dp', 'context'))
The draws below stay inside these ranges and needn't reach their ends.
All inputs are finite; a program needn't handle non-finite values.
Results may differ from the reference program's by a relative error of at most 0.0085.
Values sent between devices are 32-bit elements; how exact they have to be, the bound alone decides.
A program may use at most 64 MiB of HBM per device.

```python
import math
import jax
import jax.numpy as jnp
from jax import lax

H = 16
DH = 128
TOK_DEV = 128
LENGTH = 8192
BATCH = 8


def block_scale(key, dims, cuts, low, high):
    level, own = 1.0, jax.random.fold_in(key, 6)
    for position, parts in cuts:
        draws = jnp.exp(jax.random.uniform(jax.random.fold_in(own, position), (parts,), jnp.float32, low / len(cuts), high / len(cuts)))
        level = level * jnp.repeat(draws, dims[position] // parts).reshape([-1 if axis == position else 1 for axis in range(len(dims))])
    return level


def scatter_about(own_key, extent, scale, most, split=(), held_as=jnp.bfloat16):
    factor_of = block_scale(own_key, extent, split, -0.22, 0.18) if split else 1.0
    drawn = jax.random.normal(own_key, extent, jnp.float32) * scale * factor_of
    return jnp.minimum(jnp.maximum(drawn, -most), most).astype(held_as)


def setup_inputs(seed: int = 0) -> dict:
    splits = jax.random.split(jax.random.key(seed), 6)
    return {
        "queries": scatter_about(splits[0], (BATCH, LENGTH, H * DH), 1.0, 6.0, ((0, 8), (1, 64))),
        "key_rows": scatter_about(splits[1], (BATCH, LENGTH, H * DH), 1.0, 6.0, ((0, 8), (1, 64))),
        "value_rows": scatter_about(splits[2], (BATCH, LENGTH, H * DH), 1.0, 6.0, ((0, 8), (1, 64))),
        "out_grad": scatter_about(splits[3], (BATCH, LENGTH, H * DH), 1.0, 6.0, ((0, 8), (1, 64))),
        "feature_maps": scatter_about(splits[4], (H, DH, DH), DH ** -0.5, 0.5),
    }


HIGHEST = lax.Precision.HIGHEST

def one_sequence(queries, key_rows, value_rows, out_grad, feature_maps):
    blocks = LENGTH // TOK_DEV
    factor = 1.0 / math.sqrt(DH * LENGTH)

    def split_heads(rows):
        return rows.reshape(blocks, TOK_DEV, H, DH).astype(jnp.float32)
    maps_wide = feature_maps.astype(jnp.float32)
    query_heads = split_heads(queries)
    key_heads = split_heads(key_rows)
    value_heads = split_heads(value_rows)
    grad_heads = split_heads(out_grad)
    feat_query = jnp.einsum('nthd,hde->nhte', query_heads, maps_wide).astype(jnp.bfloat16).astype(jnp.float32)
    feat_key = jnp.einsum('nthd,hde->nhte', key_heads, maps_wide).astype(jnp.bfloat16).astype(jnp.float32)
    kv_blocks = jnp.einsum('nhsd,nshe->nhde', feat_key, value_heads)
    ga_blocks = jnp.einsum('nhtd,nthe->nhde', feat_query, grad_heads)

    def forward(running, block_term):
        return (running + block_term, running)
    empty_state = jnp.zeros((H, DH, DH), jnp.float32)
    _, prefix = lax.scan(forward, empty_state, kv_blocks)
    _, suffix = lax.scan(forward, empty_state, ga_blocks, reverse=True)
    causal = jnp.arange(TOK_DEV)[:, None] >= jnp.arange(TOK_DEV)[None, :]
    score_ab = jnp.where(causal, jnp.einsum('nhtd,nhsd->nhts', feat_query, feat_key), 0.0)
    score_ab = score_ab.astype(jnp.bfloat16).astype(jnp.float32)
    score_gv = jnp.where(causal, jnp.einsum('nthe,nshe->nhts', grad_heads, value_heads), 0.0)
    score_gv = score_gv.astype(jnp.bfloat16).astype(jnp.float32)
    feat_qgrad = factor * (jnp.einsum('nhts,nhsd->nhtd', score_gv, feat_key) + jnp.einsum('nthe,nhde->nhtd', grad_heads, prefix, precision=HIGHEST))
    feat_qgrad = feat_qgrad.astype(jnp.bfloat16).astype(jnp.float32)
    feat_kgrad = factor * (jnp.einsum('nhts,nhtd->nhsd', score_gv, feat_query) + jnp.einsum('nshe,nhde->nhsd', value_heads, suffix, precision=HIGHEST))
    feat_kgrad = feat_kgrad.astype(jnp.bfloat16).astype(jnp.float32)
    value_grad = factor * (jnp.einsum('nhts,nthe->nshe', score_ab, grad_heads) + jnp.einsum('nhsd,nhde->nshe', feat_key, suffix, precision=HIGHEST))
    query_grad = jnp.einsum('nhte,hde->nthd', feat_qgrad, maps_wide)
    key_grad = jnp.einsum('nhse,hde->nshd', feat_kgrad, maps_wide)
    maps_term = jnp.einsum('nthd,nhte->hde', query_heads, feat_qgrad) + jnp.einsum('nshd,nhse->hde', key_heads, feat_kgrad)
    return (query_grad.reshape(LENGTH, H * DH).astype(jnp.bfloat16), key_grad.reshape(LENGTH, H * DH).astype(jnp.bfloat16), value_grad.reshape(LENGTH, H * DH).astype(jnp.bfloat16), maps_term)

def reference(queries, key_rows, value_rows, out_grad, feature_maps):

    def per_sequence(inputs):
        return one_sequence(inputs[0], inputs[1], inputs[2], inputs[3], feature_maps)
    query_grad, key_grad, value_grad, maps_terms = lax.map(per_sequence, (queries, key_rows, value_rows, out_grad))
    maps_grad = lax.optimization_barrier(jnp.sum(maps_terms, axis=0)) * (1.0 / math.sqrt(BATCH * LENGTH))
    return (query_grad, key_grad, value_grad, maps_grad.reshape(H * DH, DH))
```

```python
import functools
import math

import jax
import jax.numpy as jnp
from jax import lax
from jax.experimental import pallas as pl
from jax.experimental.pallas import tpu as pltpu
from jax.sharding import PartitionSpec as P

F32, BF16 = jnp.float32, jnp.bfloat16
PIECES = 2


def nn(a, b):
    return lax.dot_general(a, b, (((1,), (0,)), ((), ())), preferred_element_type=F32)


def nt(a, b):
    return lax.dot_general(a, b, (((1,), (1,)), ((), ())), preferred_element_type=F32)


def tn(a, b):
    return lax.dot_general(a, b, (((0,), (0,)), ((), ())), preferred_element_type=F32)


def split(state):
    upper = state.astype(BF16)
    return upper, (state - upper.astype(F32)).astype(BF16)


def body(sizes, q_ref, k_ref, v_ref, g_ref, f_ref, qg_ref, kg_ref, vg_ref, mg_ref,
         a_s, b_s, state, part, base, lda, ldb, lvg, maps, peer, colbuf, rowsum, rowout, rowbuf,
         part_sem, base_sem, peer_sem, col_sem, row_sem, part_out, base_out, scan_out, peer_out, col_out, row_out):
    ndp, ny, nz, factor, norm = sizes
    tokens, width = q_ref.shape[1], f_ref.shape[1]
    unit = 2 * width
    piece = unit // PIECES
    steps, right, left = nz - 1, nz // 2, nz // 2 - 1
    per_owner = nz // ndp
    blocks = ny * nz
    d = lax.axis_index("dp")
    n = lax.axis_index("context")
    y, z = n // nz, lax.rem(n, nz)

    def at(dp, block):
        return dict(device_id=(dp, block), device_id_type=pl.DeviceIdType.MESH)

    def along(t, hops):
        return lax.rem(n + (1 - 2 * t) * hops + blocks, blocks)

    def order(t):
        return jnp.where(t == 0, n, blocks - 1 - n)

    def pair_of(r):
        return lax.rem(z + r + d * per_owner, nz)

    def rows_of(q):
        return pl.ds(q * piece, piece)

    barrier = pltpu.get_barrier_semaphore()
    for hop in (1, blocks - 1):
        pl.semaphore_signal(barrier, inc=1, **at(d, lax.rem(n + hop, blocks)))
    for i in range(1, ny):
        pl.semaphore_signal(barrier, inc=1, **at(d, lax.rem(y + i, ny) * nz + z))
    for i in range(1, nz):
        pl.semaphore_signal(barrier, inc=1, **at(d, y * nz + lax.rem(z + i, nz)))
    for i in range(1, ndp):
        pl.semaphore_signal(barrier, inc=1, **at(lax.rem(d + i, ndp), n))

    def cols(h):
        return pl.ds(pl.multiple_of(h * width, width), width)

    def head_rows(hh):
        return pl.ds(pl.multiple_of(hh * width, width), width)

    def features(i, carry):
        m, hh = i // 2, lax.rem(i, 2)
        r = jnp.where(m == nz - 1, 0, jnp.where(lax.rem(m, 2) == 0, nz - 1 - m // 2, 1 + m // 2))
        p = pair_of(r)
        h = 2 * p + hh
        fm = f_ref[h]
        a = nn(q_ref[0, :, cols(h)], fm).astype(BF16)
        b = nn(k_ref[0, :, cols(h)], fm).astype(BF16)
        a_s[h] = a
        b_s[h] = b
        state[0, p, head_rows(hh)] = tn(b, v_ref[0, :, cols(h)])
        state[1, p, head_rows(hh)] = tn(a, g_ref[0, :, cols(h)])
        return carry

    def inside(h, carry):
        causal = (lax.broadcasted_iota(jnp.int32, (tokens, tokens), 0)
                  >= lax.broadcasted_iota(jnp.int32, (tokens, tokens), 1))
        a, b = a_s[h], b_s[h]
        v, g = v_ref[0, :, cols(h)], g_ref[0, :, cols(h)]
        sab = jnp.where(causal, nt(a, b), 0.0).astype(BF16)
        sgv = jnp.where(causal, nt(g, v), 0.0).astype(BF16)
        lda[h] = nn(sgv, b)
        ldb[h] = tn(sgv, a)
        lvg[h] = tn(sab, g)
        return carry

    def part_copy(t, s, q, src):
        return pltpu.make_async_remote_copy(
            src_ref=src, dst_ref=part.at[t, s, rows_of(q)], send_sem=part_out.at[t],
            recv_sem=part_sem.at[t, s, q], **at(d, along(t, 1)))

    def base_copy(t, j, q, src, target, sem):
        return pltpu.make_async_remote_copy(
            src_ref=src, dst_ref=base.at[t, j, rows_of(q)], send_sem=sem.at[t],
            recv_sem=base_sem.at[t, j, q], **at(d, target))

    def base_wait(t, j, q):
        base_copy(t, j, q, base.at[t, j, rows_of(q)], n, base_out).wait_recv()

    lax.fori_loop(0, 4, features, 0)
    pl.semaphore_wait(barrier, 2 + (ny - 1) + (nz - 1) + (ndp - 1))
    for t in range(2):
        r = nz - 1 if t == 0 else 1
        for q in range(PIECES):
            part_copy(t, 0, q, state.at[t, pair_of(r), rows_of(q)]).start()

    def chain(s, carry):
        @pl.when(s <= nz // 2 - 1)
        def _():
            lax.fori_loop(4 * s, 4 * s + 4, features, 0)

        @pl.when(s >= nz // 2)
        def _():
            lax.fori_loop(4 * (s - nz // 2), 4 * (s - nz // 2) + 4, inside, 0)

        for q in range(PIECES):
            for t in range(2):
                p = pair_of(nz - 1 - s if t == 0 else lax.rem(1 + s, nz))
                part_copy(t, s - 1, q, part.at[t, s - 1, rows_of(q)]).wait_recv()

                @pl.when(order(t) > 0)
                def _(t=t, p=p, q=q):
                    state[t, p, rows_of(q)] += part[t, s - 1, rows_of(q)]

                @pl.when(s < steps)
                def _(t=t, p=p, q=q):
                    part_copy(t, s, q, state.at[t, p, rows_of(q)]).start()
        return carry

    lax.fori_loop(1, steps + 1, chain, 0)

    own = pair_of(0)

    def scan(i, carry):
        t = jnp.where(y < ny // 2, i, 1 - i)
        row = jnp.where(t == 0, y, ny - 1 - y)
        for q in range(PIECES):
            mine = state.at[t, own, rows_of(q)]

            @pl.when(row > 0)
            def _(q=q):
                base_wait(t, nz - 1, q)
                state[t, own, rows_of(q)] += base[t, nz - 1, rows_of(q)]

            base_copy(t, nz - 1, q, mine, along(t, nz), scan_out).start()
            base_copy(t, 0, q, mine, along(t, 1), base_out).start()

            @pl.when(row > 0)
            def _(q=q):
                base_copy(t, nz - 2, q, base.at[t, nz - 1, rows_of(q)], along(t, -1), base_out).start()
        return carry

    lax.fori_loop(0, 2, scan, 0)

    def scan_end(i, carry):
        row = jnp.where(i == 0, y, ny - 1 - y)

        @pl.when(row == 0)
        def _():
            for q in range(PIECES):
                base_wait(i, nz - 1, q)
                base_copy(i, nz - 2, q, base.at[i, nz - 1, rows_of(q)], along(i, -1), base_out).start()
        return carry

    def state_of(t, j, hh):
        from_base = jnp.where(order(t) >= j, base[t, j - 1, head_rows(hh)], 0.0)
        has_part = jnp.logical_and(order(t) > 0, j >= 2)
        slot = jnp.maximum(j - 2, 0)
        return from_base + jnp.where(has_part, part[t, slot, head_rows(hh)], 0.0)

    def finish_pair(r):
        p = pair_of(r)

        def finish(hh, carry):
            h = 2 * p + hh
            q, k = q_ref[0, :, cols(h)], k_ref[0, :, cols(h)]
            v, g = v_ref[0, :, cols(h)], g_ref[0, :, cols(h)]
            fm = f_ref[h]
            pu, plow = split(state_of(0, nz - r, hh))
            su, sl = split(state_of(1, jnp.where(r == 0, nz, r), hh))
            da = (factor * (lda[h] + (nt(g, pu) + nt(g, plow)))).astype(BF16)
            db = (factor * (ldb[h] + (nt(v, su) + nt(v, sl)))).astype(BF16)
            b = b_s[h]
            vg_ref[0, :, cols(h)] = (factor * (lvg[h] + (nn(b, su) + nn(b, sl)))).astype(BF16)
            qg_ref[0, :, cols(h)] = nt(da, fm).astype(BF16)
            kg_ref[0, :, cols(h)] = nt(db, fm).astype(BF16)
            maps[p, head_rows(hh)] = tn(q, da) + tn(k, db)
            return carry

        lax.fori_loop(0, 2, finish, 0)
        owner, place = p // per_owner, lax.rem(p, per_owner)

        @pl.when(owner != d)
        def _():
            pltpu.make_async_remote_copy(
                src_ref=maps.at[p], dst_ref=peer.at[place, d], send_sem=peer_out,
                recv_sem=peer_sem.at[place, d], **at(owner, n)).start()

    lax.fori_loop(0, 2, scan_end, 0)
    finish_pair(0)

    def spread(hop, carry):
        for q in range(PIECES):
            for t in range(2):
                base_wait(t, hop - 1, q)
                base_copy(t, hop, q, base.at[t, hop - 1, rows_of(q)], along(t, 1), base_out).start()
                base_wait(t, nz - 1 - hop, q)

                @pl.when(hop < left)
                def _(t=t, q=q):
                    base_copy(t, nz - 2 - hop, q, base.at[t, nz - 1 - hop, rows_of(q)], along(t, -1), base_out).start()

        lax.fori_loop(0, 2, lambda i, c: (finish_pair(jnp.where(i == 0, nz - hop, hop)), c)[1], 0)
        return carry

    lax.fori_loop(1, left + 1, spread, 0)
    for t in range(2):
        for q in range(PIECES):
            base_wait(t, right - 1, q)
    finish_pair(jnp.int32(nz // 2))

    for place in range(per_owner):
        mine = pl.ds(place * unit, unit)
        rowsum[mine] = maps[d * per_owner + place]
        for i in range(1, ndp):
            source = lax.rem(d + i, ndp)
            pltpu.make_async_remote_copy(
                src_ref=maps.at[0], dst_ref=peer.at[place, source], send_sem=peer_out,
                recv_sem=peer_sem.at[place, source], **at(source, n)).wait_recv()
            rowsum[mine] += peer[place, source]
    group = rowsum.shape[0] // ny
    mine = pl.ds(pl.multiple_of(y * group, group), group)
    for i in range(1, ny):
        there = lax.rem(y + i, ny)
        pltpu.make_async_remote_copy(
            src_ref=rowsum.at[pl.ds(pl.multiple_of(there * group, group), group)], dst_ref=colbuf.at[i], send_sem=col_out,
            recv_sem=col_sem.at[i], **at(d, there * nz + z)).start()
    total = rowsum[mine]
    for i in range(1, ny):
        pltpu.make_async_remote_copy(
            src_ref=colbuf.at[i], dst_ref=colbuf.at[i], send_sem=col_out,
            recv_sem=col_sem.at[i], **at(d, n)).wait_recv()
        total = total + colbuf[i]
    small = group // nz
    for i in range(nz):
        rowout[i] = total[i * small:(i + 1) * small]
    for i in range(1, nz):
        there = lax.rem(z + i, nz)
        pltpu.make_async_remote_copy(
            src_ref=rowout.at[there], dst_ref=rowbuf.at[i], send_sem=row_out,
            recv_sem=row_sem.at[i], **at(d, y * nz + there)).start()
    last = rowout[z]
    for i in range(1, nz):
        pltpu.make_async_remote_copy(
            src_ref=rowbuf.at[i], dst_ref=rowbuf.at[i], send_sem=row_out,
            recv_sem=row_sem.at[i], **at(d, n)).wait_recv()
        last = last + rowbuf[i]
    mg_ref[...] = last * norm

    def sent(ref, sem):
        pltpu.make_async_remote_copy(src_ref=ref, dst_ref=ref, send_sem=sem, recv_sem=row_sem.at[0], **at(d, n)).wait_send()

    for t in range(2):
        sent(part.at[t], part_out.at[t])
        sent(part.at[t], base_out.at[t])
        sent(state.at[t, 0], scan_out.at[t])
    sent(maps.at[pl.ds(0, nz - per_owner)], peer_out)
    sent(colbuf.at[pl.ds(1, ny - 1)], col_out)
    sent(rowbuf.at[pl.ds(1, nz - 1)], row_out)


def build(mesh, ny, nz):
    ndp = mesh.shape["dp"]

    def per_device(queries, key_rows, value_rows, out_grad, feature_maps):
        tokens = queries.shape[1]
        heads, width, _ = feature_maps.shape
        unit = 2 * width
        assert heads == 2 * nz and nz % ndp == 0 and ny * nz == mesh.shape["context"]
        per_owner = nz // ndp
        owned = per_owner * unit
        group = owned // ny
        small = group // nz
        length = tokens * ny * nz
        sizes = (ndp, ny, nz, 1.0 / math.sqrt(width * length), 1.0 / math.sqrt(ndp * length))
        dma = pltpu.SemaphoreType.DMA
        rows = jax.ShapeDtypeStruct(queries.shape, BF16)
        return pl.pallas_call(
            functools.partial(body, sizes),
            out_shape=(rows, rows, rows, jax.ShapeDtypeStruct((small, width), F32)),
            in_specs=[pl.BlockSpec(memory_space=pltpu.VMEM)] * 5,
            out_specs=(pl.BlockSpec(memory_space=pltpu.VMEM),) * 4,
            scratch_shapes=[
                pltpu.VMEM((heads, tokens, width), BF16),
                pltpu.VMEM((heads, tokens, width), BF16),
                pltpu.VMEM((2, nz, unit, width), F32),
                pltpu.VMEM((2, nz - 1, unit, width), F32),
                pltpu.VMEM((2, nz, unit, width), F32),
                pltpu.VMEM((heads, tokens, width), F32),
                pltpu.VMEM((heads, tokens, width), F32),
                pltpu.VMEM((heads, tokens, width), F32),
                pltpu.VMEM((nz, unit, width), F32),
                pltpu.VMEM((per_owner, ndp, unit, width), F32),
                pltpu.VMEM((ny, group, width), F32),
                pltpu.VMEM((owned, width), F32),
                pltpu.VMEM((nz, small, width), F32),
                pltpu.VMEM((nz, small, width), F32),
                dma((2, nz - 1, PIECES)),
                dma((2, nz, PIECES)),
                dma((per_owner, ndp)),
                dma((ny,)),
                dma((nz,)),
                dma((2,)),
                dma((2,)),
                dma((2,)),
                dma(()),
                dma(()),
                dma(()),
            ],
            compiler_params=pltpu.CompilerParams(
                collective_id=0, has_side_effects=True, vmem_limit_bytes=48 * 1024 * 1024),
        )(queries, key_rows, value_rows, out_grad, feature_maps)

    tokens_spec = P("dp", "context", None)
    return jax.shard_map(
        per_device, mesh=mesh,
        in_specs=(tokens_spec,) * 4 + (P(),),
        out_specs=(tokens_spec,) * 3 + (P(("dp", "context"), None),),
        check_vma=False)


def solution(mesh):
    return build(mesh, 8, 8)
```

```python
import functools
import math

import jax
import jax.numpy as jnp
from jax import lax
from jax.experimental import pallas as pl
from jax.experimental.pallas import tpu as pltpu
from jax.sharding import PartitionSpec as P

F32, BF16 = jnp.float32, jnp.bfloat16
PIECES = 2


def nn(a, b):
    return lax.dot_general(a, b, (((1,), (0,)), ((), ())), preferred_element_type=F32)


def nt(a, b):
    return lax.dot_general(a, b, (((1,), (1,)), ((), ())), preferred_element_type=F32)


def tn(a, b):
    return lax.dot_general(a, b, (((0,), (0,)), ((), ())), preferred_element_type=F32)


def split(state):
    upper = state.astype(BF16)
    return upper, (state - upper.astype(F32)).astype(BF16)


def body(sizes, q_ref, k_ref, v_ref, g_ref, f_ref, qg_ref, kg_ref, vg_ref, mg_ref,
         rows_s, maps_s, a_s, b_s, state, part, base, slices, sums, through, lda, ldb, lvg, maps, peer, colbuf, rowsum, rowout, rowbuf,
         rows_sem, maps_sem, part_sem, base_sem, slice_sem, sum_sem, peer_sem, col_sem, row_sem,
         part_out, base_out, slice_out, sum_out, peer_out, col_out, row_out):
    ndp, ny, nz, factor, norm = sizes
    tokens, width = q_ref.shape[1], f_ref.shape[1]
    unit = 2 * width
    piece = unit // PIECES
    steps, right, left = nz - 1, nz // 2, nz // 2 - 1
    per_owner = nz // ndp
    blocks = ny * nz
    d = lax.axis_index("dp")
    n = lax.axis_index("context")
    y, z = n // nz, lax.rem(n, nz)

    def at(dp, block):
        return dict(device_id=(dp, block), device_id_type=pl.DeviceIdType.MESH)

    def along(t, hops):
        return lax.rem(n + (1 - 2 * t) * hops + blocks, blocks)

    def order(t):
        return jnp.where(t == 0, n, blocks - 1 - n)

    def pair_of(r):
        return lax.rem(z + r + d * per_owner, nz)

    def rows_of(q):
        return pl.ds(q * piece, piece)

    barrier = pltpu.get_barrier_semaphore()
    for hop in (1, blocks - 1):
        pl.semaphore_signal(barrier, inc=1, **at(d, lax.rem(n + hop, blocks)))
    for i in range(1, ny):
        pl.semaphore_signal(barrier, inc=1, **at(d, lax.rem(y + i, ny) * nz + z))
    for i in range(1, nz):
        pl.semaphore_signal(barrier, inc=1, **at(d, y * nz + lax.rem(z + i, nz)))
    for i in range(1, ndp):
        pl.semaphore_signal(barrier, inc=1, **at(lax.rem(d + i, ndp), n))

    def pair_at(m):
        return pair_of(jnp.where(m == nz - 1, 0, jnp.where(lax.rem(m, 2) == 0, nz - 1 - m // 2, 1 + m // 2)))

    def load(m, carry):
        p = pair_at(m)
        for i, ref in enumerate((q_ref, k_ref, v_ref, g_ref)):
            pltpu.make_async_copy(ref.at[0, :, pl.ds(pl.multiple_of(p * unit, unit), unit)], rows_s.at[p, i], rows_sem.at[p]).start()
        pltpu.make_async_copy(f_ref.at[pl.ds(2 * p, 2)], maps_s.at[p], maps_sem.at[p]).start()
        return carry

    lax.fori_loop(0, nz, load, 0)

    def loaded(m, carry):
        p = pair_at(m)
        pltpu.make_async_copy(rows_s.at[p], rows_s.at[p], rows_sem.at[p]).wait()
        pltpu.make_async_copy(maps_s.at[p], maps_s.at[p], maps_sem.at[p]).wait()
        return carry

    def rows_at(i, p, hh):
        return rows_s[p, i, :, pl.ds(pl.multiple_of(hh * width, width), width)]

    def cols(h):
        return pl.ds(pl.multiple_of(h * width, width), width)

    def head_rows(hh):
        return pl.ds(pl.multiple_of(hh * width, width), width)

    def features(i, carry):
        m, hh = i // 2, lax.rem(i, 2)
        p = pair_at(m)
        h = 2 * p + hh
        fm = maps_s[p, hh]
        a = nn(rows_at(0, p, hh), fm).astype(BF16)
        b = nn(rows_at(1, p, hh), fm).astype(BF16)
        a_s[h] = a
        b_s[h] = b
        state[0, p, head_rows(hh)] = tn(b, rows_at(2, p, hh))
        state[1, p, head_rows(hh)] = tn(a, rows_at(3, p, hh))
        return carry

    def two_pairs(m):
        lax.fori_loop(m, m + 2, loaded, 0)
        lax.fori_loop(2 * m, 2 * m + 4, features, 0)

    def inside(h, carry):
        causal = (lax.broadcasted_iota(jnp.int32, (tokens, tokens), 0)
                  >= lax.broadcasted_iota(jnp.int32, (tokens, tokens), 1))
        a, b = a_s[h], b_s[h]
        p, hh = h // 2, lax.rem(h, 2)
        v, g = rows_at(2, p, hh), rows_at(3, p, hh)
        sab = jnp.where(causal, nt(a, b), 0.0).astype(BF16)
        sgv = jnp.where(causal, nt(g, v), 0.0).astype(BF16)
        lda[h] = nn(sgv, b)
        ldb[h] = tn(sgv, a)
        lvg[h] = tn(sab, g)
        return carry

    def part_copy(t, s, q, src):
        return pltpu.make_async_remote_copy(
            src_ref=src, dst_ref=part.at[t, s, rows_of(q)], send_sem=part_out.at[t],
            recv_sem=part_sem.at[t, s, q], **at(d, along(t, 1)))

    def base_copy(t, j, q, src, target, sem):
        return pltpu.make_async_remote_copy(
            src_ref=src, dst_ref=base.at[t, j, rows_of(q)], send_sem=sem.at[t],
            recv_sem=base_sem.at[t, j, q], **at(d, target))

    def base_wait(t, j, q):
        base_copy(t, j, q, base.at[t, j, rows_of(q)], n, base_out).wait_recv()

    two_pairs(0)
    pl.semaphore_wait(barrier, 2 + (ny - 1) + (nz - 1) + (ndp - 1))
    for t in range(2):
        r = nz - 1 if t == 0 else 1
        for q in range(PIECES):
            part_copy(t, 0, q, state.at[t, pair_of(r), rows_of(q)]).start()

    def chain(s, carry):
        @pl.when(s <= nz // 2 - 1)
        def _():
            two_pairs(2 * s)

        @pl.when(s >= nz // 2)
        def _():
            lax.fori_loop(4 * (s - nz // 2), 4 * (s - nz // 2) + 4, inside, 0)

        for i in range(2):
            t = jnp.where(z < nz // 2, 1 - i, i)
            p = pair_of(jnp.where(t == 0, nz - 1 - s, lax.rem(1 + s, nz)))
            for q in range(PIECES):
                part_copy(t, s - 1, q, part.at[t, s - 1, rows_of(q)]).wait_recv()

                @pl.when(order(t) > 0)
                def _(t=t, p=p, q=q):
                    state[t, p, rows_of(q)] += part[t, s - 1, rows_of(q)]

                @pl.when(s < steps)
                def _(t=t, p=p, q=q):
                    part_copy(t, s, q, state.at[t, p, rows_of(q)]).start()
        return carry

    lax.fori_loop(1, steps + 1, chain, 0)

    own = pair_of(0)
    share = unit // ny

    def share_of(row):
        return pl.ds(pl.multiple_of(row * share, share), share)

    def slice_copy(t, there, source):
        return pltpu.make_async_remote_copy(
            src_ref=state.at[t, own, share_of(there)], dst_ref=slices.at[t, source], send_sem=slice_out.at[t],
            recv_sem=slice_sem.at[t, source], **at(d, there * nz + z))

    def sum_copy(t, there, source):
        return pltpu.make_async_remote_copy(
            src_ref=sums.at[t, there], dst_ref=base.at[t, nz - 1, share_of(source)], send_sem=sum_out.at[t],
            recv_sem=sum_sem.at[t, source], **at(d, there * nz + z))

    for t in range(2):
        for i in range(1, ny):
            slice_copy(t, lax.rem(y + i, ny), y).start()
        slices[t, y] = state[t, own, share_of(y)]
    for t in range(2):
        for i in range(1, ny):
            slice_copy(t, y, lax.rem(y + i, ny)).wait_recv()
        run = slices[t, 0 if t == 0 else ny - 1]
        for i in range(1, ny):
            row = i if t == 0 else ny - 1 - i
            sums[t, row] = run
            run = run + slices[t, row]
        sums[t, 0 if t == 0 else ny - 1] = run
        for i in range(1, ny):
            sum_copy(t, lax.rem(y + i, ny), y).start()
        base[t, nz - 1, share_of(y)] = sums[t, y]
    for t in range(2):
        for i in range(1, ny):
            sum_copy(t, y, lax.rem(y + i, ny)).wait_recv()
        row = y if t == 0 else ny - 1 - y
        for q in range(PIECES):
            earlier = jnp.where(row > 0, base[t, nz - 1, rows_of(q)], 0.0)
            through[t, rows_of(q)] = state[t, own, rows_of(q)] + earlier
            base_copy(t, 0, q, through.at[t, rows_of(q)], along(t, 1), base_out).start()
            base_copy(t, nz - 2, q, base.at[t, nz - 1, rows_of(q)], along(t, -1), base_out).start()

    def state_of(t, j, hh):
        from_base = jnp.where(order(t) >= j, base[t, j - 1, head_rows(hh)], 0.0)
        has_part = jnp.logical_and(order(t) > 0, j >= 2)
        slot = jnp.maximum(j - 2, 0)
        return from_base + jnp.where(has_part, part[t, slot, head_rows(hh)], 0.0)

    def finish_pair(r):
        p = pair_of(r)

        def finish(hh, carry):
            h = 2 * p + hh
            q, k, v, g = (rows_at(i, p, hh) for i in range(4))
            fm = maps_s[p, hh]
            pu, plow = split(state_of(0, nz - r, hh))
            su, sl = split(state_of(1, jnp.where(r == 0, nz, r), hh))
            da = (factor * (lda[h] + (nt(g, pu) + nt(g, plow)))).astype(BF16)
            db = (factor * (ldb[h] + (nt(v, su) + nt(v, sl)))).astype(BF16)
            b = b_s[h]
            vg_ref[0, :, cols(h)] = (factor * (lvg[h] + (nn(b, su) + nn(b, sl)))).astype(BF16)
            qg_ref[0, :, cols(h)] = nt(da, fm).astype(BF16)
            kg_ref[0, :, cols(h)] = nt(db, fm).astype(BF16)
            maps[p, head_rows(hh)] = tn(q, da) + tn(k, db)

            @pl.when(owner != d)
            def _():
                pltpu.make_async_remote_copy(
                    src_ref=maps.at[p, head_rows(hh)], dst_ref=peer.at[place, d, head_rows(hh)], send_sem=peer_out,
                    recv_sem=peer_sem.at[place, d, hh], **at(owner, n)).start()
            return carry

        owner, place = p // per_owner, lax.rem(p, per_owner)
        lax.fori_loop(0, 2, finish, 0)

    finish_pair(0)

    def spread(hop, carry):
        for i in range(2):
            t = jnp.where(z < nz // 2, 1 - i, i)
            other = 1 - t
            for q in range(PIECES):
                base_wait(t, hop - 1, q)
                base_copy(t, hop, q, base.at[t, hop - 1, rows_of(q)], along(t, 1), base_out).start()
                base_wait(other, nz - 1 - hop, q)

                @pl.when(hop < left)
                def _(other=other, q=q):
                    base_copy(other, nz - 2 - hop, q, base.at[other, nz - 1 - hop, rows_of(q)], along(other, -1), base_out).start()

        lax.fori_loop(0, 2, lambda i, c: (finish_pair(jnp.where(i == 0, nz - hop, hop)), c)[1], 0)
        return carry

    lax.fori_loop(1, left + 1, spread, 0)
    for t in range(2):
        for q in range(PIECES):
            base_wait(t, right - 1, q)
    finish_pair(jnp.int32(nz // 2))

    for place in range(per_owner):
        mine = pl.ds(place * unit, unit)
        rowsum[mine] = maps[d * per_owner + place]
        for i in range(1, ndp):
            source = lax.rem(d + i, ndp)
            for hh in range(2):
                half = pl.ds(hh * width, width)
                pltpu.make_async_remote_copy(
                    src_ref=maps.at[0, half], dst_ref=peer.at[place, source, half], send_sem=peer_out,
                    recv_sem=peer_sem.at[place, source, hh], **at(source, n)).wait_recv()
            rowsum[mine] += peer[place, source]
    group = rowsum.shape[0] // ny
    mine = pl.ds(pl.multiple_of(y * group, group), group)
    for i in range(1, ny):
        there = lax.rem(y + i, ny)
        pltpu.make_async_remote_copy(
            src_ref=rowsum.at[pl.ds(pl.multiple_of(there * group, group), group)], dst_ref=colbuf.at[i], send_sem=col_out,
            recv_sem=col_sem.at[i], **at(d, there * nz + z)).start()
    total = rowsum[mine]
    for i in range(1, ny):
        pltpu.make_async_remote_copy(
            src_ref=colbuf.at[i], dst_ref=colbuf.at[i], send_sem=col_out,
            recv_sem=col_sem.at[i], **at(d, n)).wait_recv()
        total = total + colbuf[i]
    small = group // nz
    for i in range(nz):
        rowout[i] = total[i * small:(i + 1) * small]
    for i in range(1, nz):
        there = lax.rem(z + i, nz)
        pltpu.make_async_remote_copy(
            src_ref=rowout.at[there], dst_ref=rowbuf.at[i], send_sem=row_out,
            recv_sem=row_sem.at[i], **at(d, y * nz + there)).start()
    last = rowout[z]
    for i in range(1, nz):
        pltpu.make_async_remote_copy(
            src_ref=rowbuf.at[i], dst_ref=rowbuf.at[i], send_sem=row_out,
            recv_sem=row_sem.at[i], **at(d, n)).wait_recv()
        last = last + rowbuf[i]
    mg_ref[...] = last * norm

    def sent(ref, sem):
        pltpu.make_async_remote_copy(src_ref=ref, dst_ref=ref, send_sem=sem, recv_sem=row_sem.at[0], **at(d, n)).wait_send()

    for t in range(2):
        sent(part.at[t], part_out.at[t])
        sent(part.at[t], base_out.at[t])
        sent(slices.at[t, pl.ds(1, ny - 1)], slice_out.at[t])
        sent(sums.at[t, pl.ds(1, ny - 1)], sum_out.at[t])
    sent(maps.at[pl.ds(0, nz - per_owner)], peer_out)
    sent(colbuf.at[pl.ds(1, ny - 1)], col_out)
    sent(rowbuf.at[pl.ds(1, nz - 1)], row_out)


def build(mesh, ny, nz):
    ndp = mesh.shape["dp"]

    def per_device(queries, key_rows, value_rows, out_grad, feature_maps):
        tokens = queries.shape[1]
        heads, width, _ = feature_maps.shape
        unit = 2 * width
        assert heads == 2 * nz and nz % ndp == 0 and ny * nz == mesh.shape["context"]
        per_owner = nz // ndp
        owned = per_owner * unit
        group = owned // ny
        small = group // nz
        length = tokens * ny * nz
        sizes = (ndp, ny, nz, 1.0 / math.sqrt(width * length), 1.0 / math.sqrt(ndp * length))
        dma = pltpu.SemaphoreType.DMA
        rows = jax.ShapeDtypeStruct(queries.shape, BF16)
        return pl.pallas_call(
            functools.partial(body, sizes),
            out_shape=(rows, rows, rows, jax.ShapeDtypeStruct((small, width), F32)),
            in_specs=[pl.BlockSpec(memory_space=pl.ANY)] * 5,
            out_specs=(pl.BlockSpec(memory_space=pltpu.VMEM),) * 4,
            scratch_shapes=[
                pltpu.VMEM((nz, 4, tokens, unit), BF16),
                pltpu.VMEM((nz, 2, width, width), BF16),
                pltpu.VMEM((heads, tokens, width), BF16),
                pltpu.VMEM((heads, tokens, width), BF16),
                pltpu.VMEM((2, nz, unit, width), F32),
                pltpu.VMEM((2, nz - 1, unit, width), F32),
                pltpu.VMEM((2, nz, unit, width), F32),
                pltpu.VMEM((2, ny, unit // ny, width), F32),
                pltpu.VMEM((2, ny, unit // ny, width), F32),
                pltpu.VMEM((2, unit, width), F32),
                pltpu.VMEM((heads, tokens, width), F32),
                pltpu.VMEM((heads, tokens, width), F32),
                pltpu.VMEM((heads, tokens, width), F32),
                pltpu.VMEM((nz, unit, width), F32),
                pltpu.VMEM((per_owner, ndp, unit, width), F32),
                pltpu.VMEM((ny, group, width), F32),
                pltpu.VMEM((owned, width), F32),
                pltpu.VMEM((nz, small, width), F32),
                pltpu.VMEM((nz, small, width), F32),
                dma((nz,)),
                dma((nz,)),
                dma((2, nz - 1, PIECES)),
                dma((2, nz, PIECES)),
                dma((2, ny)),
                dma((2, ny)),
                dma((per_owner, ndp, 2)),
                dma((ny,)),
                dma((nz,)),
                dma((2,)),
                dma((2,)),
                dma((2,)),
                dma((2,)),
                dma(()),
                dma(()),
                dma(()),
            ],
            compiler_params=pltpu.CompilerParams(
                collective_id=0, has_side_effects=True, vmem_limit_bytes=62 * 1024 * 1024),
        )(queries, key_rows, value_rows, out_grad, feature_maps)

    tokens_spec = P("dp", "context", None)
    return jax.shard_map(
        per_device, mesh=mesh,
        in_specs=(tokens_spec,) * 4 + (P(),),
        out_specs=(tokens_spec,) * 3 + (P(("dp", "context"), None),),
        check_vma=False)


def solution(mesh):
    return build(mesh, 8, 8)
```

```python
import functools
import math

import jax
import jax.numpy as jnp
from jax import lax
from jax.experimental import pallas as pl
from jax.experimental.pallas import tpu as pltpu
from jax.sharding import PartitionSpec as P

F32, BF16 = jnp.float32, jnp.bfloat16
PIECES = 2


def nn(a, b):
    return lax.dot_general(a, b, (((1,), (0,)), ((), ())), preferred_element_type=F32)


def nt(a, b):
    return lax.dot_general(a, b, (((1,), (1,)), ((), ())), preferred_element_type=F32)


def tn(a, b):
    return lax.dot_general(a, b, (((0,), (0,)), ((), ())), preferred_element_type=F32)


def split(state):
    upper = state.astype(BF16)
    return upper, (state - upper.astype(F32)).astype(BF16)


def body(sizes, q_ref, k_ref, v_ref, g_ref, f_ref, qg_ref, kg_ref, vg_ref, mg_ref,
         rows_s, maps_s, a_s, b_s, state, part, first, base, slices, sums, through, lda, ldb, lvg, maps, peer, colbuf, rowsum, rowout, rowbuf,
         rows_sem, maps_sem, part_sem, first_sem, base_sem, slice_sem, sum_sem, peer_sem, col_sem, row_sem,
         part_out, base_out, slice_out, sum_out, peer_out, col_out, row_out):
    ndp, ny, nz, factor, norm = sizes
    tokens, width = q_ref.shape[1], f_ref.shape[1]
    unit = 2 * width
    piece = unit // PIECES
    right, left = nz // 2, nz // 2 - 1
    per_owner = nz // ndp
    blocks = ny * nz
    d = lax.axis_index("dp")
    n = lax.axis_index("context")
    y, z = n // nz, lax.rem(n, nz)

    def at(dp, block):
        return dict(device_id=(dp, block), device_id_type=pl.DeviceIdType.MESH)

    def along(t, hops):
        return lax.rem(n + (1 - 2 * t) * hops + blocks, blocks)

    def order(t):
        return jnp.where(t == 0, n, blocks - 1 - n)

    def pair_of(r):
        return lax.rem(z + r + d * per_owner, nz)

    def rows_of(q):
        return pl.ds(q * piece, piece)

    barrier = pltpu.get_barrier_semaphore()
    for hop in (1, blocks - 1):
        pl.semaphore_signal(barrier, inc=1, **at(d, lax.rem(n + hop, blocks)))
    for i in range(1, ny):
        pl.semaphore_signal(barrier, inc=1, **at(d, lax.rem(y + i, ny) * nz + z))
    for i in range(1, nz):
        pl.semaphore_signal(barrier, inc=1, **at(d, y * nz + lax.rem(z + i, nz)))
    for i in range(1, ndp):
        pl.semaphore_signal(barrier, inc=1, **at(lax.rem(d + i, ndp), n))

    def pair_at(m):
        return pair_of(jnp.where(lax.rem(m, 2) == 0, right + m // 2, left - m // 2))

    def load(m, carry):
        p = pair_at(m)
        for i, ref in enumerate((q_ref, k_ref, v_ref, g_ref)):
            pltpu.make_async_copy(ref.at[0, :, pl.ds(pl.multiple_of(p * unit, unit), unit)], rows_s.at[p, i], rows_sem.at[p]).start()
        pltpu.make_async_copy(f_ref.at[pl.ds(2 * p, 2)], maps_s.at[p], maps_sem.at[p]).start()
        return carry

    lax.fori_loop(0, nz, load, 0)

    def loaded(m, carry):
        p = pair_at(m)
        pltpu.make_async_copy(rows_s.at[p], rows_s.at[p], rows_sem.at[p]).wait()
        pltpu.make_async_copy(maps_s.at[p], maps_s.at[p], maps_sem.at[p]).wait()
        return carry

    def rows_at(i, p, hh):
        return rows_s[p, i, :, pl.ds(pl.multiple_of(hh * width, width), width)]

    def cols(h):
        return pl.ds(pl.multiple_of(h * width, width), width)

    def head_rows(hh):
        return pl.ds(pl.multiple_of(hh * width, width), width)

    def features(i, carry):
        m, hh = i // 2, lax.rem(i, 2)
        p = pair_at(m)
        h = 2 * p + hh
        fm = maps_s[p, hh]
        a = nn(rows_at(0, p, hh), fm).astype(BF16)
        b = nn(rows_at(1, p, hh), fm).astype(BF16)
        a_s[h] = a
        b_s[h] = b
        state[0, p, head_rows(hh)] = tn(b, rows_at(2, p, hh))
        state[1, p, head_rows(hh)] = tn(a, rows_at(3, p, hh))
        return carry

    def pairs_between(first, last):
        lax.fori_loop(first, last, loaded, 0)
        lax.fori_loop(2 * first, 2 * last, features, 0)

    def inside(i, carry):
        causal = (lax.broadcasted_iota(jnp.int32, (tokens, tokens), 0)
                  >= lax.broadcasted_iota(jnp.int32, (tokens, tokens), 1))
        p, hh = pair_at(i // 2), lax.rem(i, 2)
        h = 2 * p + hh
        a, b = a_s[h], b_s[h]
        v, g = rows_at(2, p, hh), rows_at(3, p, hh)
        sab = jnp.where(causal, nt(a, b), 0.0).astype(BF16)
        sgv = jnp.where(causal, nt(g, v), 0.0).astype(BF16)
        lda[h] = nn(sgv, b)
        ldb[h] = tn(sgv, a)
        lvg[h] = tn(sab, g)
        return carry

    def part_copy(t, slot, q, src, target):
        return pltpu.make_async_remote_copy(
            src_ref=src, dst_ref=part.at[t, slot, rows_of(q)], send_sem=part_out.at[t],
            recv_sem=part_sem.at[t, slot, q], **at(d, target))

    def first_copy(t, q, src, target):
        return pltpu.make_async_remote_copy(
            src_ref=src, dst_ref=first.at[t, rows_of(q)], send_sem=part_out.at[t],
            recv_sem=first_sem.at[t, q], **at(d, target))

    def pair_in(t, r):
        return pair_of(jnp.where(t == 0, r, nz - r))

    def send_left(t, h, q):
        src = state.at[t, pair_in(t, right + h), rows_of(q)]

        @pl.when(order(t) > 0)
        def _():
            part_copy(t, h, q, src, along(t, -1)).start()

        @pl.when(order(t) == 0)
        def _():
            first_copy(t, q, src, along(t, right + h)).start()

    def send_right(t, h, q):
        part_copy(t, right + h, q, state.at[t, pair_in(t, left - h), rows_of(q)], along(t, 1)).start()

    def base_copy(t, j, q, src, target, sem):
        return pltpu.make_async_remote_copy(
            src_ref=src, dst_ref=base.at[t, j, rows_of(q)], send_sem=sem.at[t],
            recv_sem=base_sem.at[t, j, q], **at(d, target))

    def base_wait(t, j, q):
        base_copy(t, j, q, base.at[t, j, rows_of(q)], n, base_out).wait_recv()

    pairs_between(0, 3)
    pl.semaphore_wait(barrier, 2 + (ny - 1) + (nz - 1) + (ndp - 1))
    for q in range(PIECES):
        for t in range(2):
            send_left(t, 0, q)
    for q in range(PIECES):
        for t in range(2):
            send_right(t, 0, q)

    def chain(h, carry):
        pairs_between(jnp.minimum(1 + 2 * h, nz), jnp.minimum(3 + 2 * h, nz))
        lax.fori_loop(4 * (h - 1), 4 * h, inside, 0)
        for i in range(2):
            t = jnp.where(z < nz // 2, i, 1 - i)
            for q in range(PIECES):
                p = pair_in(t, lax.rem(right + h, nz))

                @pl.when(order(t) < blocks - 1)
                def _(t=t, p=p, q=q):
                    part_copy(t, h - 1, q, part.at[t, h - 1, rows_of(q)], n).wait_recv()
                    state[t, p, rows_of(q)] += part[t, h - 1, rows_of(q)]

                @pl.when(h < right)
                def _(t=t, q=q):
                    send_left(t, h, q)

            other = 1 - t

            @pl.when(h <= left)
            def _(other=other):
                for q in range(PIECES):
                    p = pair_in(other, left - h)
                    part_copy(other, right + h - 1, q, part.at[other, right + h - 1, rows_of(q)], n).wait_recv()

                    @pl.when(order(other) > 0)
                    def _(p=p, q=q):
                        state[other, p, rows_of(q)] += part[other, right + h - 1, rows_of(q)]

                    @pl.when(h < left)
                    def _(q=q):
                        send_right(other, h, q)
        return carry

    lax.fori_loop(1, right + 1, chain, 0)
    own = pair_of(0)
    for t in range(2):
        @pl.when(jnp.logical_and(order(t) >= right, order(t) < nz))
        def _(t=t):
            for q in range(PIECES):
                first_copy(t, q, first.at[t, rows_of(q)], n).wait_recv()
                state[t, own, rows_of(q)] += first[t, rows_of(q)]

    share = unit // ny

    def share_of(row):
        return pl.ds(pl.multiple_of(row * share, share), share)

    def slice_copy(t, there, source):
        return pltpu.make_async_remote_copy(
            src_ref=state.at[t, own, share_of(there)], dst_ref=slices.at[t, source], send_sem=slice_out.at[t],
            recv_sem=slice_sem.at[t, source], **at(d, there * nz + z))

    def sum_copy(t, there, source):
        return pltpu.make_async_remote_copy(
            src_ref=sums.at[t, there], dst_ref=base.at[t, nz - 1, share_of(source)], send_sem=sum_out.at[t],
            recv_sem=sum_sem.at[t, source], **at(d, there * nz + z))

    for t in range(2):
        for i in range(1, ny):
            slice_copy(t, lax.rem(y + i, ny), y).start()
        slices[t, y] = state[t, own, share_of(y)]
    for t in range(2):
        for i in range(1, ny):
            slice_copy(t, y, lax.rem(y + i, ny)).wait_recv()
        run = slices[t, 0 if t == 0 else ny - 1]
        for i in range(1, ny):
            row = i if t == 0 else ny - 1 - i
            sums[t, row] = run
            run = run + slices[t, row]
        sums[t, 0 if t == 0 else ny - 1] = run
        for i in range(1, ny):
            sum_copy(t, lax.rem(y + i, ny), y).start()
        base[t, nz - 1, share_of(y)] = sums[t, y]
    for t in range(2):
        for i in range(1, ny):
            sum_copy(t, y, lax.rem(y + i, ny)).wait_recv()
        row = y if t == 0 else ny - 1 - y
        for q in range(PIECES):
            earlier = jnp.where(row > 0, base[t, nz - 1, rows_of(q)], 0.0)
            through[t, rows_of(q)] = state[t, own, rows_of(q)] + earlier
            base_copy(t, 0, q, through.at[t, rows_of(q)], along(t, 1), base_out).start()

            @pl.when(jnp.logical_and(order(t) >= right, order(t) < nz))
            def _(t=t, q=q):
                base[t, nz - 1, rows_of(q)] = first[t, rows_of(q)]

            base_copy(t, nz - 2, q, base.at[t, nz - 1, rows_of(q)], along(t, -1), base_out).start()

    def state_of(t, p, r, hh):
        given = base[t, nz - 1 - r, head_rows(hh)]
        ahead = jnp.where(order(t) > 0, given - state[t, p, head_rows(hh)], 0.0)
        chained = part[t, right + jnp.maximum(left - 1 - r, 0), head_rows(hh)]
        has_chained = jnp.logical_and(order(t) > 0, r < left)
        behind = jnp.where(order(t) + r >= right, given, 0.0) + jnp.where(has_chained, chained, 0.0)
        return jnp.where(r >= right, ahead, behind)

    def finish_pair(r):
        p = pair_of(r)

        def finish(hh, carry):
            h = 2 * p + hh
            q, k, v, g = (rows_at(i, p, hh) for i in range(4))
            fm = maps_s[p, hh]
            pu, plow = split(state_of(0, p, r, hh))
            su, sl = split(state_of(1, p, lax.rem(nz - r, nz), hh))
            da = (factor * (lda[h] + (nt(g, pu) + nt(g, plow)))).astype(BF16)
            db = (factor * (ldb[h] + (nt(v, su) + nt(v, sl)))).astype(BF16)
            b = b_s[h]
            vg_ref[0, :, cols(h)] = (factor * (lvg[h] + (nn(b, su) + nn(b, sl)))).astype(BF16)
            qg_ref[0, :, cols(h)] = nt(da, fm).astype(BF16)
            kg_ref[0, :, cols(h)] = nt(db, fm).astype(BF16)
            maps[p, head_rows(hh)] = tn(q, da) + tn(k, db)

            @pl.when(owner != d)
            def _():
                pltpu.make_async_remote_copy(
                    src_ref=maps.at[p, head_rows(hh)], dst_ref=peer.at[place, d, head_rows(hh)], send_sem=peer_out,
                    recv_sem=peer_sem.at[place, d, hh], **at(owner, n)).start()
            return carry

        owner, place = p // per_owner, lax.rem(p, per_owner)
        lax.fori_loop(0, 2, finish, 0)

    finish_pair(jnp.int32(0))

    def spread(hop, carry):
        for i in range(2):
            t = jnp.where(z < nz // 2, 1 - i, i)
            other = 1 - t
            for q in range(PIECES):
                base_wait(t, hop - 1, q)

                @pl.when(order(t) > 0)
                def _(t=t, q=q):
                    base_copy(t, hop, q, base.at[t, hop - 1, rows_of(q)], along(t, 1), base_out).start()

                @pl.when(order(t) == 0)
                def _(t=t, q=q):
                    base_copy(t, hop, q, state.at[t, pair_in(t, nz - hop), rows_of(q)], along(t, 1), base_out).start()

                base_wait(other, nz - 1 - hop, q)

                @pl.when(hop < left)
                def _(other=other, q=q):
                    base_copy(other, nz - 2 - hop, q, base.at[other, nz - 1 - hop, rows_of(q)], along(other, -1), base_out).start()

        lax.fori_loop(0, 2, lambda i, c: (finish_pair(jnp.where(i == 0, nz - hop, hop)), c)[1], 0)
        return carry

    lax.fori_loop(1, left + 1, spread, 0)
    for t in range(2):
        for q in range(PIECES):
            base_wait(t, right - 1, q)
    finish_pair(jnp.int32(nz // 2))

    for place in range(per_owner):
        mine = pl.ds(place * unit, unit)
        rowsum[mine] = maps[d * per_owner + place]
        for i in range(1, ndp):
            source = lax.rem(d + i, ndp)
            for hh in range(2):
                half = pl.ds(hh * width, width)
                pltpu.make_async_remote_copy(
                    src_ref=maps.at[0, half], dst_ref=peer.at[place, source, half], send_sem=peer_out,
                    recv_sem=peer_sem.at[place, source, hh], **at(source, n)).wait_recv()
            rowsum[mine] += peer[place, source]
    group = rowsum.shape[0] // ny
    mine = pl.ds(pl.multiple_of(y * group, group), group)
    for i in range(1, ny):
        there = lax.rem(y + i, ny)
        pltpu.make_async_remote_copy(
            src_ref=rowsum.at[pl.ds(pl.multiple_of(there * group, group), group)], dst_ref=colbuf.at[i], send_sem=col_out,
            recv_sem=col_sem.at[i], **at(d, there * nz + z)).start()
    total = rowsum[mine]
    for i in range(1, ny):
        pltpu.make_async_remote_copy(
            src_ref=colbuf.at[i], dst_ref=colbuf.at[i], send_sem=col_out,
            recv_sem=col_sem.at[i], **at(d, n)).wait_recv()
        total = total + colbuf[i]
    small = group // nz
    for i in range(nz):
        rowout[i] = total[i * small:(i + 1) * small]
    for i in range(1, nz):
        there = lax.rem(z + i, nz)
        pltpu.make_async_remote_copy(
            src_ref=rowout.at[there], dst_ref=rowbuf.at[i], send_sem=row_out,
            recv_sem=row_sem.at[i], **at(d, y * nz + there)).start()
    last = rowout[z]
    for i in range(1, nz):
        pltpu.make_async_remote_copy(
            src_ref=rowbuf.at[i], dst_ref=rowbuf.at[i], send_sem=row_out,
            recv_sem=row_sem.at[i], **at(d, n)).wait_recv()
        last = last + rowbuf[i]
    mg_ref[...] = last * norm

    def sent(ref, sem):
        pltpu.make_async_remote_copy(src_ref=ref, dst_ref=ref, send_sem=sem, recv_sem=row_sem.at[0], **at(d, n)).wait_send()

    for t in range(2):
        sent(part.at[t], part_out.at[t])
        sent(part.at[t], base_out.at[t])
        sent(slices.at[t, pl.ds(1, ny - 1)], slice_out.at[t])
        sent(sums.at[t, pl.ds(1, ny - 1)], sum_out.at[t])
    sent(maps.at[pl.ds(0, nz - per_owner)], peer_out)
    sent(colbuf.at[pl.ds(1, ny - 1)], col_out)
    sent(rowbuf.at[pl.ds(1, nz - 1)], row_out)


def write_out(*refs):
    sems = refs[8]
    copies = [pltpu.make_async_copy(refs[i], refs[4 + i], sems.at[i]) for i in range(4)]
    for copy in copies:
        copy.start()
    for copy in copies:
        copy.wait()


def build(mesh, ny, nz):
    ndp = mesh.shape["dp"]

    def per_device(queries, key_rows, value_rows, out_grad, feature_maps):
        tokens = queries.shape[1]
        heads, width, _ = feature_maps.shape
        unit = 2 * width
        assert heads == 2 * nz and nz % ndp == 0 and ny * nz == mesh.shape["context"]
        per_owner = nz // ndp
        owned = per_owner * unit
        group = owned // ny
        small = group // nz
        length = tokens * ny * nz
        sizes = (ndp, ny, nz, 1.0 / math.sqrt(width * length), 1.0 / math.sqrt(ndp * length))
        dma = pltpu.SemaphoreType.DMA
        rows = jax.ShapeDtypeStruct(queries.shape, BF16)
        results = pl.pallas_call(
            functools.partial(body, sizes),
            out_shape=(rows, rows, rows, jax.ShapeDtypeStruct((small, width), F32)),
            in_specs=[pl.BlockSpec(memory_space=pltpu.HBM)] * 5,
            out_specs=(pl.BlockSpec(memory_space=pltpu.VMEM),) * 4,
            scratch_shapes=[
                pltpu.VMEM((nz, 4, tokens, unit), BF16),
                pltpu.VMEM((nz, 2, width, width), BF16),
                pltpu.VMEM((heads, tokens, width), BF16),
                pltpu.VMEM((heads, tokens, width), BF16),
                pltpu.VMEM((2, nz, unit, width), F32),
                pltpu.VMEM((2, nz - 1, unit, width), F32),
                pltpu.VMEM((2, unit, width), F32),
                pltpu.VMEM((2, nz, unit, width), F32),
                pltpu.VMEM((2, ny, unit // ny, width), F32),
                pltpu.VMEM((2, ny, unit // ny, width), F32),
                pltpu.VMEM((2, unit, width), F32),
                pltpu.VMEM((heads, tokens, width), F32),
                pltpu.VMEM((heads, tokens, width), F32),
                pltpu.VMEM((heads, tokens, width), F32),
                pltpu.VMEM((nz, unit, width), F32),
                pltpu.VMEM((per_owner, ndp, unit, width), F32),
                pltpu.VMEM((ny, group, width), F32),
                pltpu.VMEM((owned, width), F32),
                pltpu.VMEM((nz, small, width), F32),
                pltpu.VMEM((nz, small, width), F32),
                dma((nz,)),
                dma((nz,)),
                dma((2, nz - 1, PIECES)),
                dma((2, PIECES)),
                dma((2, nz, PIECES)),
                dma((2, ny)),
                dma((2, ny)),
                dma((per_owner, ndp, 2)),
                dma((ny,)),
                dma((nz,)),
                dma((2,)),
                dma((2,)),
                dma((2,)),
                dma((2,)),
                dma(()),
                dma(()),
                dma(()),
            ],
            compiler_params=pltpu.CompilerParams(
                collective_id=0, has_side_effects=True, vmem_limit_bytes=62 * 1024 * 1024),
        )(queries, key_rows, value_rows, out_grad, feature_maps)
        return pl.pallas_call(
            write_out,
            out_shape=tuple(jax.ShapeDtypeStruct(x.shape, x.dtype) for x in results),
            in_specs=[pl.BlockSpec(memory_space=pltpu.VMEM)] * 4,
            out_specs=(pl.BlockSpec(memory_space=pltpu.HBM),) * 4,
            scratch_shapes=[dma((4,))],
        )(*results)

    tokens_spec = P("dp", "context", None)
    return jax.shard_map(
        per_device, mesh=mesh,
        in_specs=(tokens_spec,) * 4 + (P(),),
        out_specs=(tokens_spec,) * 3 + (P(("dp", "context"), None),),
        check_vma=False)


def solution(mesh):
    return build(mesh, 8, 8)
```

```python
import functools
import math

import jax
import jax.numpy as jnp
from jax import lax
from jax.experimental import pallas as pl
from jax.experimental.pallas import tpu as pltpu
from jax.sharding import PartitionSpec as P

F32, BF16 = jnp.float32, jnp.bfloat16
PIECES = 2
BANDS = 4


def nn(a, b):
    return lax.dot_general(a, b, (((1,), (0,)), ((), ())), preferred_element_type=F32)


def nt(a, b):
    return lax.dot_general(a, b, (((1,), (1,)), ((), ())), preferred_element_type=F32)


def tn(a, b):
    return lax.dot_general(a, b, (((0,), (0,)), ((), ())), preferred_element_type=F32)


def split(state):
    upper = state.astype(BF16)
    return upper, (state - upper.astype(F32)).astype(BF16)


def body(sizes, q_ref, k_ref, v_ref, g_ref, f_ref, qg_ref, kg_ref, vg_ref, mg_ref,
         rows_s, maps_s, a_s, b_s, state, part, first, base, slices, sums, through, lda, ldb, lvg, maps, peer, colbuf, rowsum, rowout, rowbuf, da_s, db_s, out_s,
         rows_sem, maps_sem, part_sem, first_sem, base_sem, slice_sem, sum_sem, peer_sem, col_sem, row_sem,
         part_out, base_out, slice_out, sum_out, peer_out, col_out, row_out, out_sem):
    ndp, ny, nz, factor, norm = sizes
    tokens, width = q_ref.shape[1], f_ref.shape[1]
    unit = 2 * width
    piece = unit // PIECES
    right, left = nz // 2, nz // 2 - 1
    per_owner = nz // ndp
    blocks = ny * nz
    d = lax.axis_index("dp")
    n = lax.axis_index("context")
    y, z = n // nz, lax.rem(n, nz)

    def at(dp, block):
        return dict(device_id=(dp, block), device_id_type=pl.DeviceIdType.MESH)

    def along(t, hops):
        return lax.rem(n + (1 - 2 * t) * hops + blocks, blocks)

    def order(t):
        return jnp.where(t == 0, n, blocks - 1 - n)

    def pair_of(r):
        return lax.rem(z + r + d * per_owner, nz)

    def rows_of(q):
        return pl.ds(q * piece, piece)

    barrier = pltpu.get_barrier_semaphore()
    for hop in (1, blocks - 1):
        pl.semaphore_signal(barrier, inc=1, **at(d, lax.rem(n + hop, blocks)))
    for i in range(1, ny):
        pl.semaphore_signal(barrier, inc=1, **at(d, lax.rem(y + i, ny) * nz + z))
    for i in range(1, nz):
        pl.semaphore_signal(barrier, inc=1, **at(d, y * nz + lax.rem(z + i, nz)))
    for i in range(1, ndp):
        pl.semaphore_signal(barrier, inc=1, **at(lax.rem(d + i, ndp), n))

    def pair_at(m):
        return pair_of(jnp.where(lax.rem(m, 2) == 0, right + m // 2, left - m // 2))

    def load(m, carry):
        p = pair_at(m)
        for i, ref in enumerate((q_ref, k_ref, v_ref, g_ref)):
            pltpu.make_async_copy(ref.at[0, :, pl.ds(pl.multiple_of(p * unit, unit), unit)], rows_s.at[p, i], rows_sem.at[p]).start()
        pltpu.make_async_copy(f_ref.at[pl.ds(2 * p, 2)], maps_s.at[p], maps_sem.at[p]).start()
        return carry

    lax.fori_loop(0, nz, load, 0)

    def loaded(m, carry):
        p = pair_at(m)
        pltpu.make_async_copy(rows_s.at[p], rows_s.at[p], rows_sem.at[p]).wait()
        pltpu.make_async_copy(maps_s.at[p], maps_s.at[p], maps_sem.at[p]).wait()
        return carry

    def rows_at(i, p, hh):
        return rows_s[p, i, :, pl.ds(pl.multiple_of(hh * width, width), width)]

    def cols(h):
        return pl.ds(pl.multiple_of(h * width, width), width)

    def head_rows(hh):
        return pl.ds(pl.multiple_of(hh * width, width), width)

    def features(i, carry):
        m, hh = i // 2, lax.rem(i, 2)
        p = pair_at(m)
        h = 2 * p + hh
        fm = maps_s[p, hh]
        a = nn(rows_at(0, p, hh), fm).astype(BF16)
        b = nn(rows_at(1, p, hh), fm).astype(BF16)
        a_s[h] = a
        b_s[h] = b
        state[0, p, head_rows(hh)] = tn(b, rows_at(2, p, hh))
        state[1, p, head_rows(hh)] = tn(a, rows_at(3, p, hh))
        return carry

    def pairs_between(first, last):
        lax.fori_loop(first, last, loaded, 0)
        lax.fori_loop(2 * first, 2 * last, features, 0)

    def inside(i, carry):
        causal = (lax.broadcasted_iota(jnp.int32, (tokens, tokens), 0)
                  >= lax.broadcasted_iota(jnp.int32, (tokens, tokens), 1))
        p, hh = pair_at(i // 2), lax.rem(i, 2)
        h = 2 * p + hh
        a, b = a_s[h], b_s[h]
        v, g = rows_at(2, p, hh), rows_at(3, p, hh)
        sab = jnp.where(causal, nt(a, b), 0.0).astype(BF16)
        sgv = jnp.where(causal, nt(g, v), 0.0).astype(BF16)
        lda[h] = nn(sgv, b)
        ldb[h] = tn(sgv, a)
        lvg[h] = tn(sab, g)
        return carry

    def part_copy(t, slot, q, src, target):
        return pltpu.make_async_remote_copy(
            src_ref=src, dst_ref=part.at[t, slot, rows_of(q)], send_sem=part_out.at[t],
            recv_sem=part_sem.at[t, slot, q], **at(d, target))

    def first_copy(t, q, src, target):
        return pltpu.make_async_remote_copy(
            src_ref=src, dst_ref=first.at[t, rows_of(q)], send_sem=part_out.at[t],
            recv_sem=first_sem.at[t, q], **at(d, target))

    def pair_in(t, r):
        return pair_of(jnp.where(t == 0, r, nz - r))

    def send_left(t, h, q):
        src = state.at[t, pair_in(t, right + h), rows_of(q)]

        @pl.when(order(t) > 0)
        def _():
            part_copy(t, h, q, src, along(t, -1)).start()

        @pl.when(order(t) == 0)
        def _():
            first_copy(t, q, src, along(t, right + h)).start()

    def send_right(t, h, q):
        part_copy(t, right + h, q, state.at[t, pair_in(t, left - h), rows_of(q)], along(t, 1)).start()

    def base_copy(t, j, q, src, target, sem):
        return pltpu.make_async_remote_copy(
            src_ref=src, dst_ref=base.at[t, j, rows_of(q)], send_sem=sem.at[t],
            recv_sem=base_sem.at[t, j, q], **at(d, target))

    def base_wait(t, j, q):
        base_copy(t, j, q, base.at[t, j, rows_of(q)], n, base_out).wait_recv()

    pairs_between(0, 1)
    pl.semaphore_wait(barrier, 2 + (ny - 1) + (nz - 1) + (ndp - 1))
    for q in range(PIECES):
        for t in range(2):
            send_left(t, 0, q)
    pairs_between(1, 3)
    for q in range(PIECES):
        for t in range(2):
            send_right(t, 0, q)

    def chain(h, carry):
        pairs_between(jnp.minimum(1 + 2 * h, nz), jnp.minimum(3 + 2 * h, nz))
        lax.fori_loop(4 * (h - 1), 4 * h, inside, 0)
        for i in range(2):
            t = jnp.where(z < nz // 2, i, 1 - i)
            for q in range(PIECES):
                p = pair_in(t, lax.rem(right + h, nz))

                @pl.when(order(t) < blocks - 1)
                def _(t=t, p=p, q=q):
                    part_copy(t, h - 1, q, part.at[t, h - 1, rows_of(q)], n).wait_recv()
                    state[t, p, rows_of(q)] += part[t, h - 1, rows_of(q)]

                @pl.when(h < right)
                def _(t=t, q=q):
                    send_left(t, h, q)

            other = 1 - t

            @pl.when(h <= left)
            def _(other=other):
                for q in range(PIECES):
                    p = pair_in(other, left - h)
                    part_copy(other, right + h - 1, q, part.at[other, right + h - 1, rows_of(q)], n).wait_recv()

                    @pl.when(order(other) > 0)
                    def _(p=p, q=q):
                        state[other, p, rows_of(q)] += part[other, right + h - 1, rows_of(q)]

                    @pl.when(h < left)
                    def _(q=q):
                        send_right(other, h, q)
        return carry

    lax.fori_loop(1, right + 1, chain, 0)
    own = pair_of(0)
    for t in range(2):
        @pl.when(jnp.logical_and(order(t) >= right, order(t) < nz))
        def _(t=t):
            for q in range(PIECES):
                first_copy(t, q, first.at[t, rows_of(q)], n).wait_recv()
                state[t, own, rows_of(q)] += first[t, rows_of(q)]

    share = unit // ny

    def share_of(row):
        return pl.ds(pl.multiple_of(row * share, share), share)

    def slice_copy(t, there, source):
        return pltpu.make_async_remote_copy(
            src_ref=state.at[t, own, share_of(there)], dst_ref=slices.at[t, source], send_sem=slice_out.at[t],
            recv_sem=slice_sem.at[t, source], **at(d, there * nz + z))

    def sum_copy(t, there, source):
        return pltpu.make_async_remote_copy(
            src_ref=sums.at[t, there], dst_ref=base.at[t, nz - 1, share_of(source)], send_sem=sum_out.at[t],
            recv_sem=sum_sem.at[t, source], **at(d, there * nz + z))

    for t in range(2):
        for i in range(1, ny):
            slice_copy(t, lax.rem(y + i, ny), y).start()
        slices[t, y] = state[t, own, share_of(y)]
    for t in range(2):
        for i in range(1, ny):
            slice_copy(t, y, lax.rem(y + i, ny)).wait_recv()
        run = slices[t, 0 if t == 0 else ny - 1]
        for i in range(1, ny):
            row = i if t == 0 else ny - 1 - i
            sums[t, row] = run
            run = run + slices[t, row]
        sums[t, 0 if t == 0 else ny - 1] = run
        for i in range(1, ny):
            sum_copy(t, lax.rem(y + i, ny), y).start()
        base[t, nz - 1, share_of(y)] = sums[t, y]
    for t in range(2):
        for i in range(1, ny):
            sum_copy(t, y, lax.rem(y + i, ny)).wait_recv()
        row = y if t == 0 else ny - 1 - y
        for q in range(PIECES):
            earlier = jnp.where(row > 0, base[t, nz - 1, rows_of(q)], 0.0)
            through[t, rows_of(q)] = state[t, own, rows_of(q)] + earlier
            base_copy(t, 0, q, through.at[t, rows_of(q)], along(t, 1), base_out).start()

            @pl.when(jnp.logical_and(order(t) >= right, order(t) < nz))
            def _(t=t, q=q):
                base[t, nz - 1, rows_of(q)] = first[t, rows_of(q)]

            base_copy(t, nz - 2, q, base.at[t, nz - 1, rows_of(q)], along(t, -1), base_out).start()

    def state_of(t, p, r, hh):
        given = base[t, nz - 1 - r, head_rows(hh)]
        ahead = jnp.where(order(t) > 0, given - state[t, p, head_rows(hh)], 0.0)
        chained = part[t, right + jnp.maximum(left - 1 - r, 0), head_rows(hh)]
        has_chained = jnp.logical_and(order(t) > 0, r < left)
        behind = jnp.where(order(t) + r >= right, given, 0.0) + jnp.where(has_chained, chained, 0.0)
        return jnp.where(r >= right, ahead, behind)

    def finish_pair(r):
        p = pair_of(r)

        def gradients(hh, carry):
            h = 2 * p + hh
            q, k, v, g = (rows_at(i, p, hh) for i in range(4))
            pu, plow = split(state_of(0, p, r, hh))
            su, sl = split(state_of(1, p, lax.rem(nz - r, nz), hh))
            da = (factor * (lda[h] + (nt(g, pu) + nt(g, plow)))).astype(BF16)
            db = (factor * (ldb[h] + (nt(v, su) + nt(v, sl)))).astype(BF16)
            da_s[hh] = da
            db_s[hh] = db
            maps[p, head_rows(hh)] = tn(q, da) + tn(k, db)

            @pl.when(owner != d)
            def _():
                pltpu.make_async_remote_copy(
                    src_ref=maps.at[p, head_rows(hh)], dst_ref=peer.at[place, d, head_rows(hh)], send_sem=peer_out,
                    recv_sem=peer_sem.at[place, d, hh], **at(owner, n)).start()
            return carry

        def outputs(hh, carry):
            h = 2 * p + hh
            fm = maps_s[p, hh]
            su, sl = split(state_of(1, p, lax.rem(nz - r, nz), hh))
            b = b_s[h]
            mine = pl.ds(pl.multiple_of(hh * width, width), width)
            out_s[p, 0, :, mine] = nt(da_s[hh], fm).astype(BF16)
            out_s[p, 1, :, mine] = nt(db_s[hh], fm).astype(BF16)
            out_s[p, 2, :, mine] = (factor * (lvg[h] + (nn(b, su) + nn(b, sl)))).astype(BF16)
            return carry

        owner, place = p // per_owner, lax.rem(p, per_owner)
        lax.fori_loop(0, 2, gradients, 0)
        lax.fori_loop(0, 2, outputs, 0)
        for i, ref in enumerate((qg_ref, kg_ref, vg_ref)):
            pltpu.make_async_copy(out_s.at[p, i], ref.at[0, :, pl.ds(pl.multiple_of(p * unit, unit), unit)], out_sem).start()

    finish_pair(jnp.int32(0))

    def spread(hop, carry):
        for i in range(2):
            t = jnp.where(z < nz // 2, 1 - i, i)
            other = 1 - t
            for q in range(PIECES):
                base_wait(t, hop - 1, q)

                @pl.when(order(t) > 0)
                def _(t=t, q=q):
                    base_copy(t, hop, q, base.at[t, hop - 1, rows_of(q)], along(t, 1), base_out).start()

                @pl.when(order(t) == 0)
                def _(t=t, q=q):
                    base_copy(t, hop, q, state.at[t, pair_in(t, nz - hop), rows_of(q)], along(t, 1), base_out).start()

                base_wait(other, nz - 1 - hop, q)

                @pl.when(hop < left)
                def _(other=other, q=q):
                    base_copy(other, nz - 2 - hop, q, base.at[other, nz - 1 - hop, rows_of(q)], along(other, -1), base_out).start()

        lax.fori_loop(0, 2, lambda i, c: (finish_pair(jnp.where(i == 0, nz - hop, hop)), c)[1], 0)
        return carry

    lax.fori_loop(1, left + 1, spread, 0)
    for t in range(2):
        for q in range(PIECES):
            base_wait(t, right - 1, q)
    finish_pair(jnp.int32(nz // 2))

    for place in range(per_owner):
        mine = pl.ds(place * unit, unit)
        rowsum[mine] = maps[d * per_owner + place]
        for i in range(1, ndp):
            source = lax.rem(d + i, ndp)
            for hh in range(2):
                half = pl.ds(hh * width, width)
                pltpu.make_async_remote_copy(
                    src_ref=maps.at[0, half], dst_ref=peer.at[place, source, half], send_sem=peer_out,
                    recv_sem=peer_sem.at[place, source, hh], **at(source, n)).wait_recv()
            rowsum[mine] += peer[place, source]
    group = rowsum.shape[0] // ny
    mine = pl.ds(pl.multiple_of(y * group, group), group)
    for i in range(1, ny):
        there = lax.rem(y + i, ny)
        pltpu.make_async_remote_copy(
            src_ref=rowsum.at[pl.ds(pl.multiple_of(there * group, group), group)], dst_ref=colbuf.at[i], send_sem=col_out,
            recv_sem=col_sem.at[i], **at(d, there * nz + z)).start()
    total = rowsum[mine]
    for i in range(1, ny):
        pltpu.make_async_remote_copy(
            src_ref=colbuf.at[i], dst_ref=colbuf.at[i], send_sem=col_out,
            recv_sem=col_sem.at[i], **at(d, n)).wait_recv()
        total = total + colbuf[i]
    small = group // nz
    for i in range(nz):
        rowout[i] = total[i * small:(i + 1) * small]
    for i in range(1, nz):
        there = lax.rem(z + i, nz)
        pltpu.make_async_remote_copy(
            src_ref=rowout.at[there], dst_ref=rowbuf.at[i], send_sem=row_out,
            recv_sem=row_sem.at[i], **at(d, y * nz + there)).start()
    last = rowout[z]
    for i in range(1, nz):
        pltpu.make_async_remote_copy(
            src_ref=rowbuf.at[i], dst_ref=rowbuf.at[i], send_sem=row_out,
            recv_sem=row_sem.at[i], **at(d, n)).wait_recv()
        last = last + rowbuf[i]
    mg_ref[...] = last * norm

    pltpu.make_async_copy(out_s, out_s, out_sem).wait()

    def sent(ref, sem):
        pltpu.make_async_remote_copy(src_ref=ref, dst_ref=ref, send_sem=sem, recv_sem=row_sem.at[0], **at(d, n)).wait_send()

    for t in range(2):
        sent(part.at[t], part_out.at[t])
        sent(part.at[t], base_out.at[t])
        sent(slices.at[t, pl.ds(1, ny - 1)], slice_out.at[t])
        sent(sums.at[t, pl.ds(1, ny - 1)], sum_out.at[t])
    sent(maps.at[pl.ds(0, nz - per_owner)], peer_out)
    sent(colbuf.at[pl.ds(1, ny - 1)], col_out)
    sent(rowbuf.at[pl.ds(1, nz - 1)], row_out)


def write_out(*refs):
    held, small, in_sem, out_sem = refs[8:]
    rows = held.shape[1] // BANDS
    bands = [(i, pl.ds(j * rows, rows), i * BANDS + j) for i in range(3) for j in range(BANDS)]
    fetch = [pltpu.make_async_copy(refs[i].at[0, band], held.at[i, band], in_sem.at[k]) for i, band, k in bands]
    store = [pltpu.make_async_copy(held.at[i, band], refs[4 + i].at[0, band], out_sem.at[k]) for i, band, k in bands]
    fetch.append(pltpu.make_async_copy(refs[3], small, in_sem.at[3 * BANDS]))
    store.append(pltpu.make_async_copy(small, refs[7], out_sem.at[3 * BANDS]))
    for copy in fetch:
        copy.start()
    for arrived, copy in zip(fetch, store):
        arrived.wait()
        copy.start()
    for copy in store:
        copy.wait()


def build(mesh, ny, nz):
    ndp = mesh.shape["dp"]

    def per_device(queries, key_rows, value_rows, out_grad, feature_maps):
        tokens = queries.shape[1]
        heads, width, _ = feature_maps.shape
        unit = 2 * width
        assert heads == 2 * nz and nz % ndp == 0 and ny * nz == mesh.shape["context"]
        per_owner = nz // ndp
        owned = per_owner * unit
        group = owned // ny
        small = group // nz
        length = tokens * ny * nz
        sizes = (ndp, ny, nz, 1.0 / math.sqrt(width * length), 1.0 / math.sqrt(ndp * length))
        dma = pltpu.SemaphoreType.DMA
        rows = jax.ShapeDtypeStruct(queries.shape, BF16)
        results = pl.pallas_call(
            functools.partial(body, sizes),
            out_shape=(rows, rows, rows, jax.ShapeDtypeStruct((small, width), F32)),
            in_specs=[pl.BlockSpec(memory_space=pl.ANY)] * 5,
            out_specs=(pl.BlockSpec(memory_space=pl.ANY),) * 3 + (pl.BlockSpec(memory_space=pltpu.VMEM),),
            scratch_shapes=[
                pltpu.VMEM((nz, 4, tokens, unit), BF16),
                pltpu.VMEM((nz, 2, width, width), BF16),
                pltpu.VMEM((heads, tokens, width), BF16),
                pltpu.VMEM((heads, tokens, width), BF16),
                pltpu.VMEM((2, nz, unit, width), F32),
                pltpu.VMEM((2, nz - 1, unit, width), F32),
                pltpu.VMEM((2, unit, width), F32),
                pltpu.VMEM((2, nz, unit, width), F32),
                pltpu.VMEM((2, ny, unit // ny, width), F32),
                pltpu.VMEM((2, ny, unit // ny, width), F32),
                pltpu.VMEM((2, unit, width), F32),
                pltpu.VMEM((heads, tokens, width), F32),
                pltpu.VMEM((heads, tokens, width), F32),
                pltpu.VMEM((heads, tokens, width), F32),
                pltpu.VMEM((nz, unit, width), F32),
                pltpu.VMEM((per_owner, ndp, unit, width), F32),
                pltpu.VMEM((ny, group, width), F32),
                pltpu.VMEM((owned, width), F32),
                pltpu.VMEM((nz, small, width), F32),
                pltpu.VMEM((nz, small, width), F32),
                pltpu.VMEM((2, tokens, width), BF16),
                pltpu.VMEM((2, tokens, width), BF16),
                pltpu.VMEM((nz, 3, tokens, unit), BF16),
                dma((nz,)),
                dma((nz,)),
                dma((2, nz - 1, PIECES)),
                dma((2, PIECES)),
                dma((2, nz, PIECES)),
                dma((2, ny)),
                dma((2, ny)),
                dma((per_owner, ndp, 2)),
                dma((ny,)),
                dma((nz,)),
                dma((2,)),
                dma((2,)),
                dma((2,)),
                dma((2,)),
                dma(()),
                dma(()),
                dma(()),
                dma(()),
            ],
            compiler_params=pltpu.CompilerParams(
                collective_id=0, has_side_effects=True, vmem_limit_bytes=62 * 1024 * 1024),
        )(queries, key_rows, value_rows, out_grad, feature_maps)
        return pl.pallas_call(
            write_out,
            out_shape=tuple(jax.ShapeDtypeStruct(x.shape, x.dtype) for x in results),
            in_specs=[pl.BlockSpec(memory_space=pl.ANY)] * 4,
            out_specs=(pl.BlockSpec(memory_space=pl.ANY),) * 4,
            scratch_shapes=[
                pltpu.VMEM((3,) + queries.shape[1:], BF16),
                pltpu.VMEM((small, width), F32),
                dma((3 * BANDS + 1,)),
                dma((3 * BANDS + 1,)),
            ],
            compiler_params=pltpu.CompilerParams(vmem_limit_bytes=62 * 1024 * 1024),
        )(*results)

    tokens_spec = P("dp", "context", None)
    return jax.shard_map(
        per_device, mesh=mesh,
        in_specs=(tokens_spec,) * 4 + (P(),),
        out_specs=(tokens_spec,) * 3 + (P(("dp", "context"), None),),
        check_vma=False)


def solution(mesh):
    return build(mesh, 8, 8)
```

```python
import functools
import math

import jax
import jax.numpy as jnp
from jax import lax
from jax.experimental import pallas as pl
from jax.experimental.pallas import tpu as pltpu
from jax.sharding import PartitionSpec as P

F32, BF16 = jnp.float32, jnp.bfloat16
PIECES = 1
BANDS = 4


def nn(a, b):
    return lax.dot_general(a, b, (((1,), (0,)), ((), ())), preferred_element_type=F32)


def nt(a, b):
    return lax.dot_general(a, b, (((1,), (1,)), ((), ())), preferred_element_type=F32)


def tn(a, b):
    return lax.dot_general(a, b, (((0,), (0,)), ((), ())), preferred_element_type=F32)


def split(state):
    upper = state.astype(BF16)
    return upper, (state - upper.astype(F32)).astype(BF16)


def body(sizes, q_ref, k_ref, v_ref, g_ref, f_ref, qg_ref, kg_ref, vg_ref, mg_ref,
         rows_s, maps_s, a_s, b_s, state, part, first, base, slices, sums, through, lda, ldb, lvg, maps, peer, colbuf, rowsum, rowout, rowbuf, da_s, db_s, out_s,
         rows_sem, maps_sem, part_sem, first_sem, base_sem, slice_sem, sum_sem, peer_sem, col_sem, row_sem,
         part_out, base_out, slice_out, sum_out, peer_out, col_out, row_out, out_sem):
    ndp, ny, nz, factor, norm = sizes
    tokens, width = q_ref.shape[1], f_ref.shape[1]
    unit = 2 * width
    piece = unit // PIECES
    right, left = nz // 2, nz // 2 - 1
    per_owner = nz // ndp
    blocks = ny * nz
    d = lax.axis_index("dp")
    n = lax.axis_index("context")
    y, z = n // nz, lax.rem(n, nz)

    def at(dp, block):
        return dict(device_id=(dp, block), device_id_type=pl.DeviceIdType.MESH)

    def along(t, hops):
        return lax.rem(n + (1 - 2 * t) * hops + blocks, blocks)

    def order(t):
        return jnp.where(t == 0, n, blocks - 1 - n)

    def pair_of(r):
        return lax.rem(z + r + d * per_owner, nz)

    def rows_of(q):
        return pl.ds(q * piece, piece)

    barrier = pltpu.get_barrier_semaphore()
    for hop in (1, blocks - 1):
        pl.semaphore_signal(barrier, inc=1, **at(d, lax.rem(n + hop, blocks)))
    for i in range(1, ny):
        pl.semaphore_signal(barrier, inc=1, **at(d, lax.rem(y + i, ny) * nz + z))
    for i in range(1, nz):
        pl.semaphore_signal(barrier, inc=1, **at(d, y * nz + lax.rem(z + i, nz)))
    for i in range(1, ndp):
        pl.semaphore_signal(barrier, inc=1, **at(lax.rem(d + i, ndp), n))

    def pair_at(m):
        return pair_of(jnp.where(lax.rem(m, 2) == 0, right + m // 2, left - m // 2))

    def load(m, carry):
        p = pair_at(m)
        for i, ref in enumerate((q_ref, k_ref, v_ref, g_ref)):
            pltpu.make_async_copy(ref.at[0, :, pl.ds(pl.multiple_of(p * unit, unit), unit)], rows_s.at[p, i], rows_sem.at[p]).start()
        pltpu.make_async_copy(f_ref.at[pl.ds(2 * p, 2)], maps_s.at[p], maps_sem.at[p]).start()
        return carry

    lax.fori_loop(0, nz, load, 0)

    def loaded(m, carry):
        p = pair_at(m)
        pltpu.make_async_copy(rows_s.at[p], rows_s.at[p], rows_sem.at[p]).wait()
        pltpu.make_async_copy(maps_s.at[p], maps_s.at[p], maps_sem.at[p]).wait()
        return carry

    def rows_at(i, p, hh):
        return rows_s[p, i, :, pl.ds(pl.multiple_of(hh * width, width), width)]

    def cols(h):
        return pl.ds(pl.multiple_of(h * width, width), width)

    def head_rows(hh):
        return pl.ds(pl.multiple_of(hh * width, width), width)

    def features(i, carry):
        m, hh = i // 2, lax.rem(i, 2)
        p = pair_at(m)
        h = 2 * p + hh
        fm = maps_s[p, hh]
        a = nn(rows_at(0, p, hh), fm).astype(BF16)
        b = nn(rows_at(1, p, hh), fm).astype(BF16)
        a_s[h] = a
        b_s[h] = b
        state[0, p, head_rows(hh)] = tn(b, rows_at(2, p, hh))
        state[1, p, head_rows(hh)] = tn(a, rows_at(3, p, hh))
        return carry

    def pairs_between(first, last):
        lax.fori_loop(first, last, loaded, 0)
        lax.fori_loop(2 * first, 2 * last, features, 0)

    def inside(i, carry):
        causal = (lax.broadcasted_iota(jnp.int32, (tokens, tokens), 0)
                  >= lax.broadcasted_iota(jnp.int32, (tokens, tokens), 1))
        p, hh = pair_at(i // 2), lax.rem(i, 2)
        h = 2 * p + hh
        a, b = a_s[h], b_s[h]
        v, g = rows_at(2, p, hh), rows_at(3, p, hh)
        sab = jnp.where(causal, nt(a, b), 0.0).astype(BF16)
        sgv = jnp.where(causal, nt(g, v), 0.0).astype(BF16)
        lda[h] = nn(sgv, b)
        ldb[h] = tn(sgv, a)
        lvg[h] = tn(sab, g)
        return carry

    def part_copy(t, slot, q, src, target):
        return pltpu.make_async_remote_copy(
            src_ref=src, dst_ref=part.at[t, slot, rows_of(q)], send_sem=part_out.at[t],
            recv_sem=part_sem.at[t, slot, q], **at(d, target))

    def first_copy(t, q, src, target):
        return pltpu.make_async_remote_copy(
            src_ref=src, dst_ref=first.at[t, rows_of(q)], send_sem=part_out.at[t],
            recv_sem=first_sem.at[t, q], **at(d, target))

    def pair_in(t, r):
        return pair_of(jnp.where(t == 0, r, nz - r))

    def send_left(t, h, q):
        src = state.at[t, pair_in(t, right + h), rows_of(q)]

        @pl.when(order(t) > 0)
        def _():
            part_copy(t, h, q, src, along(t, -1)).start()

        @pl.when(order(t) == 0)
        def _():
            first_copy(t, q, src, along(t, right + h)).start()

    def send_right(t, h, q):
        part_copy(t, right + h, q, state.at[t, pair_in(t, left - h), rows_of(q)], along(t, 1)).start()

    def base_copy(t, j, q, src, target, sem):
        return pltpu.make_async_remote_copy(
            src_ref=src, dst_ref=base.at[t, j, rows_of(q)], send_sem=sem.at[t],
            recv_sem=base_sem.at[t, j, q], **at(d, target))

    def base_wait(t, j, q):
        base_copy(t, j, q, base.at[t, j, rows_of(q)], n, base_out).wait_recv()

    pairs_between(0, 1)
    pl.semaphore_wait(barrier, 2 + (ny - 1) + (nz - 1) + (ndp - 1))
    for q in range(PIECES):
        for t in range(2):
            send_left(t, 0, q)
    pairs_between(1, 3)
    for q in range(PIECES):
        for t in range(2):
            send_right(t, 0, q)

    def chain(h, carry):
        pairs_between(jnp.minimum(1 + 2 * h, nz), jnp.minimum(3 + 2 * h, nz))
        lax.fori_loop(4 * (h - 1), 4 * h, inside, 0)
        for i in range(2):
            t = jnp.where(z < nz // 2, i, 1 - i)
            for q in range(PIECES):
                p = pair_in(t, lax.rem(right + h, nz))

                @pl.when(order(t) < blocks - 1)
                def _(t=t, p=p, q=q):
                    part_copy(t, h - 1, q, part.at[t, h - 1, rows_of(q)], n).wait_recv()
                    state[t, p, rows_of(q)] += part[t, h - 1, rows_of(q)]

                @pl.when(h < right)
                def _(t=t, q=q):
                    send_left(t, h, q)

            other = 1 - t

            @pl.when(h <= left)
            def _(other=other):
                for q in range(PIECES):
                    p = pair_in(other, left - h)
                    part_copy(other, right + h - 1, q, part.at[other, right + h - 1, rows_of(q)], n).wait_recv()

                    @pl.when(order(other) > 0)
                    def _(p=p, q=q):
                        state[other, p, rows_of(q)] += part[other, right + h - 1, rows_of(q)]

                    @pl.when(h < left)
                    def _(q=q):
                        send_right(other, h, q)
        return carry

    lax.fori_loop(1, right + 1, chain, 0)
    own = pair_of(0)
    for t in range(2):
        @pl.when(jnp.logical_and(order(t) >= right, order(t) < nz))
        def _(t=t):
            for q in range(PIECES):
                first_copy(t, q, first.at[t, rows_of(q)], n).wait_recv()
                state[t, own, rows_of(q)] += first[t, rows_of(q)]

    share = unit // ny

    def share_of(row):
        return pl.ds(pl.multiple_of(row * share, share), share)

    def slice_copy(t, there, source):
        return pltpu.make_async_remote_copy(
            src_ref=state.at[t, own, share_of(there)], dst_ref=slices.at[t, source], send_sem=slice_out.at[t],
            recv_sem=slice_sem.at[t, source], **at(d, there * nz + z))

    def sum_copy(t, there, source):
        return pltpu.make_async_remote_copy(
            src_ref=sums.at[t, there], dst_ref=base.at[t, nz - 1, share_of(source)], send_sem=sum_out.at[t],
            recv_sem=sum_sem.at[t, source], **at(d, there * nz + z))

    far_first = sorted(range(1, ny), key=lambda i: -min(i, ny - i))
    for t in range(2):
        for i in far_first:
            slice_copy(t, lax.rem(y + i, ny), y).start()
        slices[t, y] = state[t, own, share_of(y)]
    for t in range(2):
        for i in range(1, ny):
            slice_copy(t, y, lax.rem(y + i, ny)).wait_recv()
        run = slices[t, 0 if t == 0 else ny - 1]
        for i in range(1, ny):
            row = i if t == 0 else ny - 1 - i
            sums[t, row] = run
            run = run + slices[t, row]
        sums[t, 0 if t == 0 else ny - 1] = run
        for i in far_first:
            sum_copy(t, lax.rem(y + i, ny), y).start()
        base[t, nz - 1, share_of(y)] = sums[t, y]
    for t in range(2):
        row = y if t == 0 else ny - 1 - y
        for q in range(PIECES):
            for source in range(q * ny // PIECES, (q + 1) * ny // PIECES):
                @pl.when(source != y)
                def _(t=t, source=source):
                    sum_copy(t, y, source).wait_recv()

            earlier = jnp.where(row > 0, base[t, nz - 1, rows_of(q)], 0.0)
            through[t, rows_of(q)] = state[t, own, rows_of(q)] + earlier
            base_copy(t, 0, q, through.at[t, rows_of(q)], along(t, 1), base_out).start()

            @pl.when(jnp.logical_and(order(t) >= right, order(t) < nz))
            def _(t=t, q=q):
                base[t, nz - 1, rows_of(q)] = first[t, rows_of(q)]

            base_copy(t, nz - 2, q, base.at[t, nz - 1, rows_of(q)], along(t, -1), base_out).start()

    def state_of(t, p, r, hh):
        given = base[t, nz - 1 - r, head_rows(hh)]
        ahead = jnp.where(order(t) > 0, given - state[t, p, head_rows(hh)], 0.0)
        chained = part[t, right + jnp.maximum(left - 1 - r, 0), head_rows(hh)]
        has_chained = jnp.logical_and(order(t) > 0, r < left)
        behind = jnp.where(order(t) + r >= right, given, 0.0) + jnp.where(has_chained, chained, 0.0)
        return jnp.where(r >= right, ahead, behind)

    def finish_pair(r):
        p = pair_of(r)

        def gradients(hh, carry):
            h = 2 * p + hh
            q, k, v, g = (rows_at(i, p, hh) for i in range(4))
            pu, plow = split(state_of(0, p, r, hh))
            su, sl = split(state_of(1, p, lax.rem(nz - r, nz), hh))
            da = (factor * (lda[h] + (nt(g, pu) + nt(g, plow)))).astype(BF16)
            db = (factor * (ldb[h] + (nt(v, su) + nt(v, sl)))).astype(BF16)
            da_s[hh] = da
            db_s[hh] = db
            maps[p, head_rows(hh)] = tn(q, da) + tn(k, db)

            @pl.when(owner != d)
            def _():
                pltpu.make_async_remote_copy(
                    src_ref=maps.at[p, head_rows(hh)], dst_ref=peer.at[place, d, head_rows(hh)], send_sem=peer_out,
                    recv_sem=peer_sem.at[place, d, hh], **at(owner, n)).start()
            return carry

        def outputs(hh, carry):
            h = 2 * p + hh
            fm = maps_s[p, hh]
            su, sl = split(state_of(1, p, lax.rem(nz - r, nz), hh))
            b = b_s[h]
            mine = pl.ds(pl.multiple_of(hh * width, width), width)
            out_s[p, 0, :, mine] = nt(da_s[hh], fm).astype(BF16)
            out_s[p, 1, :, mine] = nt(db_s[hh], fm).astype(BF16)
            out_s[p, 2, :, mine] = (factor * (lvg[h] + (nn(b, su) + nn(b, sl)))).astype(BF16)
            return carry

        owner, place = p // per_owner, lax.rem(p, per_owner)
        lax.fori_loop(0, 2, gradients, 0)
        lax.fori_loop(0, 2, outputs, 0)
        for i, ref in enumerate((qg_ref, kg_ref, vg_ref)):
            pltpu.make_async_copy(out_s.at[p, i], ref.at[0, :, pl.ds(pl.multiple_of(p * unit, unit), unit)], out_sem).start()

    finish_pair(jnp.int32(0))

    def spread(hop, carry):
        for i in range(2):
            t = jnp.where(z < nz // 2, 1 - i, i)
            other = 1 - t
            for q in range(PIECES):
                base_wait(t, hop - 1, q)

                @pl.when(order(t) > 0)
                def _(t=t, q=q):
                    base_copy(t, hop, q, base.at[t, hop - 1, rows_of(q)], along(t, 1), base_out).start()

                @pl.when(order(t) == 0)
                def _(t=t, q=q):
                    base_copy(t, hop, q, state.at[t, pair_in(t, nz - hop), rows_of(q)], along(t, 1), base_out).start()

                base_wait(other, nz - 1 - hop, q)

                @pl.when(hop < left)
                def _(other=other, q=q):
                    base_copy(other, nz - 2 - hop, q, base.at[other, nz - 1 - hop, rows_of(q)], along(other, -1), base_out).start()

        lax.fori_loop(0, 2, lambda i, c: (finish_pair(jnp.where(i == 0, nz - hop, hop)), c)[1], 0)
        return carry

    lax.fori_loop(1, left + 1, spread, 0)
    for t in range(2):
        for q in range(PIECES):
            base_wait(t, right - 1, q)
    finish_pair(jnp.int32(nz // 2))

    for place in range(per_owner):
        mine = pl.ds(place * unit, unit)
        rowsum[mine] = maps[d * per_owner + place]
        for i in range(1, ndp):
            source = lax.rem(d + i, ndp)
            for hh in range(2):
                half = pl.ds(hh * width, width)
                pltpu.make_async_remote_copy(
                    src_ref=maps.at[0, half], dst_ref=peer.at[place, source, half], send_sem=peer_out,
                    recv_sem=peer_sem.at[place, source, hh], **at(source, n)).wait_recv()
            rowsum[mine] += peer[place, source]
    group = rowsum.shape[0] // ny
    mine = pl.ds(pl.multiple_of(y * group, group), group)
    for i in far_first:
        there = lax.rem(y + i, ny)
        pltpu.make_async_remote_copy(
            src_ref=rowsum.at[pl.ds(pl.multiple_of(there * group, group), group)], dst_ref=colbuf.at[i], send_sem=col_out,
            recv_sem=col_sem.at[i], **at(d, there * nz + z)).start()
    total = rowsum[mine]
    for i in range(1, ny):
        pltpu.make_async_remote_copy(
            src_ref=colbuf.at[i], dst_ref=colbuf.at[i], send_sem=col_out,
            recv_sem=col_sem.at[i], **at(d, n)).wait_recv()
        total = total + colbuf[i]
    small = group // nz
    for i in range(nz):
        rowout[i] = total[i * small:(i + 1) * small]
    for i in sorted(range(1, nz), key=lambda i: -min(i, nz - i)):
        there = lax.rem(z + i, nz)
        pltpu.make_async_remote_copy(
            src_ref=rowout.at[there], dst_ref=rowbuf.at[i], send_sem=row_out,
            recv_sem=row_sem.at[i], **at(d, y * nz + there)).start()
    last = rowout[z]
    for i in range(1, nz):
        pltpu.make_async_remote_copy(
            src_ref=rowbuf.at[i], dst_ref=rowbuf.at[i], send_sem=row_out,
            recv_sem=row_sem.at[i], **at(d, n)).wait_recv()
        last = last + rowbuf[i]
    mg_ref[...] = last * norm

    pltpu.make_async_copy(out_s, out_s, out_sem).wait()

    def sent(ref, sem):
        pltpu.make_async_remote_copy(src_ref=ref, dst_ref=ref, send_sem=sem, recv_sem=row_sem.at[0], **at(d, n)).wait_send()

    for t in range(2):
        sent(part.at[t], part_out.at[t])
        sent(part.at[t], base_out.at[t])
        sent(slices.at[t, pl.ds(1, ny - 1)], slice_out.at[t])
        sent(sums.at[t, pl.ds(1, ny - 1)], sum_out.at[t])
    sent(maps.at[pl.ds(0, nz - per_owner)], peer_out)
    sent(colbuf.at[pl.ds(1, ny - 1)], col_out)
    sent(rowbuf.at[pl.ds(1, nz - 1)], row_out)


def write_out(*refs):
    held, small, in_sem, out_sem = refs[8:]
    rows = held.shape[1] // BANDS
    bands = [(i, pl.ds(j * rows, rows), i * BANDS + j) for i in range(3) for j in range(BANDS)]
    fetch = [pltpu.make_async_copy(refs[i].at[0, band], held.at[i, band], in_sem.at[k]) for i, band, k in bands]
    store = [pltpu.make_async_copy(held.at[i, band], refs[4 + i].at[0, band], out_sem.at[k]) for i, band, k in bands]
    fetch.append(pltpu.make_async_copy(refs[3], small, in_sem.at[3 * BANDS]))
    store.append(pltpu.make_async_copy(small, refs[7], out_sem.at[3 * BANDS]))
    for copy in fetch:
        copy.start()
    for arrived, copy in zip(fetch, store):
        arrived.wait()
        copy.start()
    for copy in store:
        copy.wait()


def build(mesh, ny, nz):
    ndp = mesh.shape["dp"]

    def per_device(queries, key_rows, value_rows, out_grad, feature_maps):
        tokens = queries.shape[1]
        heads, width, _ = feature_maps.shape
        unit = 2 * width
        assert heads == 2 * nz and nz % ndp == 0 and ny * nz == mesh.shape["context"]
        per_owner = nz // ndp
        owned = per_owner * unit
        group = owned // ny
        small = group // nz
        length = tokens * ny * nz
        sizes = (ndp, ny, nz, 1.0 / math.sqrt(width * length), 1.0 / math.sqrt(ndp * length))
        dma = pltpu.SemaphoreType.DMA
        rows = jax.ShapeDtypeStruct(queries.shape, BF16)
        results = pl.pallas_call(
            functools.partial(body, sizes),
            out_shape=(rows, rows, rows, jax.ShapeDtypeStruct((small, width), F32)),
            in_specs=[pl.BlockSpec(memory_space=pl.ANY)] * 5,
            out_specs=(pl.BlockSpec(memory_space=pl.ANY),) * 3 + (pl.BlockSpec(memory_space=pltpu.VMEM),),
            scratch_shapes=[
                pltpu.VMEM((nz, 4, tokens, unit), BF16),
                pltpu.VMEM((nz, 2, width, width), BF16),
                pltpu.VMEM((heads, tokens, width), BF16),
                pltpu.VMEM((heads, tokens, width), BF16),
                pltpu.VMEM((2, nz, unit, width), F32),
                pltpu.VMEM((2, nz - 1, unit, width), F32),
                pltpu.VMEM((2, unit, width), F32),
                pltpu.VMEM((2, nz, unit, width), F32),
                pltpu.VMEM((2, ny, unit // ny, width), F32),
                pltpu.VMEM((2, ny, unit // ny, width), F32),
                pltpu.VMEM((2, unit, width), F32),
                pltpu.VMEM((heads, tokens, width), F32),
                pltpu.VMEM((heads, tokens, width), F32),
                pltpu.VMEM((heads, tokens, width), F32),
                pltpu.VMEM((nz, unit, width), F32),
                pltpu.VMEM((per_owner, ndp, unit, width), F32),
                pltpu.VMEM((ny, group, width), F32),
                pltpu.VMEM((owned, width), F32),
                pltpu.VMEM((nz, small, width), F32),
                pltpu.VMEM((nz, small, width), F32),
                pltpu.VMEM((2, tokens, width), BF16),
                pltpu.VMEM((2, tokens, width), BF16),
                pltpu.VMEM((nz, 3, tokens, unit), BF16),
                dma((nz,)),
                dma((nz,)),
                dma((2, nz - 1, PIECES)),
                dma((2, PIECES)),
                dma((2, nz, PIECES)),
                dma((2, ny)),
                dma((2, ny)),
                dma((per_owner, ndp, 2)),
                dma((ny,)),
                dma((nz,)),
                dma((2,)),
                dma((2,)),
                dma((2,)),
                dma((2,)),
                dma(()),
                dma(()),
                dma(()),
                dma(()),
            ],
            compiler_params=pltpu.CompilerParams(
                collective_id=0, has_side_effects=True, vmem_limit_bytes=62 * 1024 * 1024),
        )(queries, key_rows, value_rows, out_grad, feature_maps)
        return pl.pallas_call(
            write_out,
            out_shape=tuple(jax.ShapeDtypeStruct(x.shape, x.dtype) for x in results),
            in_specs=[pl.BlockSpec(memory_space=pl.ANY)] * 4,
            out_specs=(pl.BlockSpec(memory_space=pl.ANY),) * 4,
            scratch_shapes=[
                pltpu.VMEM((3,) + queries.shape[1:], BF16),
                pltpu.VMEM((small, width), F32),
                dma((3 * BANDS + 1,)),
                dma((3 * BANDS + 1,)),
            ],
            compiler_params=pltpu.CompilerParams(vmem_limit_bytes=62 * 1024 * 1024),
        )(*results)

    tokens_spec = P("dp", "context", None)
    return jax.shard_map(
        per_device, mesh=mesh,
        in_specs=(tokens_spec,) * 4 + (P(),),
        out_specs=(tokens_spec,) * 3 + (P(("dp", "context"), None),),
        check_vma=False)


def solution(mesh):
    return build(mesh, 8, 8)
```
